512 devices in a mesh: gx: 8 (over z_hi, core), gy: 16 (over z_lo, x), gz: 4 (over y).
Axes of the slice: x: 4, y: 4, z: 16 (z_hi: 4, z_lo: 4; z = z_hi * 4 + z_lo), core: 2. Of those that a mesh axis runs over, the one named last changes fastest.
Arguments:
- cr_init: float32 [64, 16, 32, 2048], P(None, 'gz', 'gx', 'gy'), may hold values from 0.1 to 3
- gas: float32 [16, 32, 2048], P('gz', 'gx', 'gy'), may hold values from 0.05 to 3
- diff_coeff: float32 [64], replicated, may hold values from 0.06 to 0.14
- loss_coeff: float32 [64], replicated, may hold values from 0.05 to 0.3
- pi0_table: float32 [96, 64], replicated, may hold values from -0.75 to 0.75
- los_weight: bfloat16 [4, 8, 16, 7, 2048, 128], P('gz', 'gx', 'gy'), may hold values from -0.125 to 0.125
- slot_owner: int32 [4, 8, 16, 7, 1], P('gz', 'gx', 'gy'), may hold values from 0 to 15; in each aligned block of 7 rows (0 to 6, 7 to 13, ..., all dimensions but the last counted through in order) at most 2 rows name the same one
- slot_block: int32 [4, 8, 16, 7], P('gz', 'gx', 'gy'), may hold values from 0 to 3
Outputs:
- cr_final: float32 [64, 16, 32, 2048], P(None, 'gz', 'gx', 'gy')
- sky: float32 [4, 8, 64, 96, 128], P('gz', 'gx', 'gy')
The draws below stay inside these ranges and needn't reach their ends.
Inputs may be any that keep to these rules, and one draw needn't show every extreme that they name: `slot_owner`: at most 2 of the 7 weight blocks of one device name the same owner, and some device names one owner exactly 2 times.
All inputs are finite; a program needn't handle non-finite values.
Results may differ from the reference program's by a relative error of at most 0.0029.
Values sent between devices are 32-bit elements; how exact they have to be, the bound alone decides.
No kernel may reach another device: no remote copies, remote signals or barrier semaphores. Data moves between devices by JAX's collectives and lax.ppermute only.
A program may use at most 64 MiB of HBM per device.

```python
import math
import jax
import jax.numpy as jnp
import numpy as np
from jax import lax

NE = 64
NG = 96
PB = 128
CX = 4
CY = 128
CZ = 4
STEPS = 2
KS = 7
BO = 4
CAP = 2
CELLS = 2048
NX = 32
NY = 2048
NZ = 16
N_GX = 8
N_GY = 16
N_GZ = 4


def draw_cr_init(key, part):
    key_base = jax.random.fold_in(key, 11)
    key_high = jax.random.fold_in(key, 12)
    shape = (NE, NZ, NX, NY)
    base = jnp.exp(jax.random.uniform(key_base, shape, jnp.float32, math.log(0.1), math.log(0.3)))
    high = jnp.exp(jax.random.uniform(key_high, shape, jnp.float32, math.log(1.0), math.log(3.0)))
    place = jnp.arange(NY) % CY
    second = (place == 1) | (place == CY - 2)
    return jnp.where(second[None, None, None, :], high, base).astype(jnp.float32)


def draw_gas(key, part):
    key_base = jax.random.fold_in(key, 21)
    key_face = jax.random.fold_in(key, 22)
    shape = (NZ, NX, NY)
    base = jnp.exp(jax.random.uniform(key_base, shape, jnp.float32, math.log(0.05), math.log(0.15)))
    face = jnp.exp(jax.random.uniform(key_face, shape, jnp.float32, math.log(1.0), math.log(3.0)))
    place = jnp.arange(NY) % CY
    outer = (place == 0) | (place == CY - 1)
    return jnp.where(outer[None, None, :], face, base).astype(jnp.float32)


def plant(entries, rng, smallest, largest):
    longest = entries.shape.index(max(entries.shape))
    spots = []
    for shift in (0, 1):
        where = [jax.random.randint(jax.random.fold_in(rng, axis), (), 0, length) for axis, length in enumerate(entries.shape)]
        where[longest] = (where[longest] + shift) % entries.shape[longest]
        spots.append(tuple(where))
    return entries.at[spots[0]].set(smallest).at[spots[1]].set(largest)


def steps_of(key, dims, cuts, low, high):
    gain = 1.0
    for position, parts in cuts:
        draws = jax.random.uniform(jax.random.fold_in(jax.random.fold_in(key, 6), position), (parts,), jnp.float32, low / len(cuts), high / len(cuts))
        gain = gain * jnp.repeat(jnp.exp(draws), dims[position] // parts).reshape((-1,) + (1,) * (len(dims) - 1 - position))
    return gain


def shared_out(own_key, own, number, rows, amount, top, bound, skew):
    sequence = jax.random.permutation(own_key, amount)
    crowded, common = portions_of(amount, rows * top, bound, skew, True), portions_of(amount, rows * top, bound, skew, False)
    places = jnp.arange(amount)

    def named(sizes, offset_by):
        used = int((sizes > 0).sum())
        fixed = max(1, used // 4)
        moved = fixed + (places - fixed + offset_by * (used - fixed)) % max(1, amount - fixed)
        return jnp.zeros((amount,), jnp.int32).at[sequence[jnp.where(places < fixed, places, moved)]].set(jnp.asarray(sizes, jnp.int32))

    sizes = jnp.where(number % 4 == 0, named(crowded, number // 4), named(common, number - number // 4 - 1))
    mixed = jax.random.permutation(jax.random.fold_in(own, 3), amount)
    source_of, taker = mixed[0:amount // 2 * 2:2], mixed[1:amount // 2 * 2:2]
    room = jnp.minimum(sizes[source_of] - 1, bound - sizes[taker]) // 2
    room = jnp.where((source_of == sequence[0]) | (taker == sequence[0]) | (sizes[taker] == 0), 0, jnp.maximum(room, 0))
    moved = jax.random.randint(jax.random.fold_in(own, 4), (amount // 2,), 0, 1 << 20) % (room + 1)
    sizes = sizes.at[source_of].add(-moved).at[taker].add(moved)
    labels = jnp.searchsorted(jnp.cumsum(sizes), jnp.arange(rows * top), side="right").astype(jnp.int32)
    grid = labels.reshape(top, rows).T
    grid = grid[jax.random.permutation(jax.random.fold_in(own, 1), rows)]
    offset_by = jax.random.randint(jax.random.fold_in(own, 2), (rows, 1), 0, top)
    return jnp.take_along_axis(grid, (jnp.arange(top)[None, :] + offset_by) % top, axis=1)


def portions_of(count, total, limit, skew, full):
    portions = [(1 << 20) // math.isqrt(grade ** skew) + 1 for grade in range(1, count + 1)]
    largest = limit if full else min(limit, max(-(-total // count), total * portions[0] // sum(portions)))
    least = 1 if total - largest >= count - 1 else 0
    holding, spare = [largest] + [least] * (count - 1), total - largest - least * (count - 1)
    while spare > 0:
        free = [i for i in range(1, count) if holding[i] < largest] or [i for i in range(1, count) if holding[i] < limit]
        pool, left = sum([portions[i] for i in free]), spare
        for i in free:
            more = min(limit - holding[i], max(1, left * portions[i] // pool), spare)
            holding[i] = holding[i] + more
            spare = spare - more
    return np.array(holding)


def normal_values(rng, extent, scale, most, split=(), dtype=jnp.bfloat16):
    array = scale * jax.random.normal(rng, extent, jnp.float32)
    if split:
        array = array * steps_of(rng, extent, split, -0.22, 0.18)
    return jnp.clip(array, -most, most).astype(dtype)


def setup_inputs(seed: int = 0) -> dict:
    key_list = jax.random.split(jax.random.key(seed), 9)
    cr_init = draw_cr_init(jax.random.fold_in(key_list[8], 71), 0)
    gas = draw_gas(jax.random.fold_in(key_list[8], 71), 0)
    diff_coeff = jnp.clip(jax.random.uniform(key_list[2], (NE,), jnp.float32, 0.06, 0.14), 0.06, 0.14)
    loss_coeff = jnp.clip(jnp.exp(jax.random.uniform(key_list[3], (NE,), jnp.float32, math.log(0.05), math.log(0.3))), 0.05, 0.3)
    pi0_table = normal_values(key_list[4], (NG, NE), NE ** -0.5, 0.75, (), jnp.float32)
    los_weight = normal_values(key_list[5], (N_GZ, N_GX, N_GY, KS, CELLS, PB), CELLS ** -0.5, 0.125, ((0, 4), (1, 8), (2, 16)))
    slot_owner_keys = jax.random.split(jax.random.fold_in(key_list[6], 1), N_GZ * N_GX * N_GY * KS // KS)
    slot_owner_turns = jax.random.permutation(jax.random.fold_in(key_list[6], 3), N_GZ * N_GX * N_GY * KS // KS)
    slot_owner = jax.vmap(lambda own, number: shared_out(jax.random.fold_in(key_list[6], 2), own, number, KS, N_GY, 1, CAP, 2))(slot_owner_keys, slot_owner_turns).reshape((N_GZ, N_GX, N_GY, KS, 1))
    slot_block = plant(jax.random.randint(key_list[7], (N_GZ, N_GX, N_GY, KS), 0, BO), jax.random.fold_in(key_list[7], 1), 0, BO - 1).astype(jnp.int32)
    return {"cr_init": cr_init, "gas": gas, "diff_coeff": diff_coeff, "loss_coeff": loss_coeff, "pi0_table": pi0_table, "los_weight": los_weight, "slot_owner": slot_owner, "slot_block": slot_block}


def advance(padded, diffusion, losses):
    center = padded[:, 1:-1, 1:-1, 1:-1]
    beside = padded[:, 2:, 1:-1, 1:-1] + padded[:, :-2, 1:-1, 1:-1]
    beside = beside + padded[:, 1:-1, 2:, 1:-1] + padded[:, 1:-1, :-2, 1:-1]
    beside = beside + padded[:, 1:-1, 1:-1, 2:] + padded[:, 1:-1, 1:-1, :-2]
    loss_flux = losses[:, None, None, None] * center
    from_above = jnp.concatenate([loss_flux[1:], jnp.zeros_like(loss_flux[:1])], axis=0)
    return center + diffusion[:, None, None, None] * (beside - 6.0 * center) + from_above - loss_flux


def reference(cr_init, gas, diff_coeff, loss_coeff, pi0_table, los_weight, slot_owner, slot_block):
    density = cr_init
    for step_index in range(STEPS):
        padded = jnp.pad(density, ((0, 0), (1, 1), (1, 1), (1, 1)))
        density = advance(padded, diff_coeff, loss_coeff)
    source = jnp.einsum("ge,ezxy->gzxy", pi0_table, density, precision=lax.Precision.HIGHEST)
    emissivity = (gas[None] * source).astype(jnp.bfloat16)
    tile_rows = emissivity.reshape(NG, N_GZ, CZ, N_GX, CX, N_GY, CY)
    tile_rows = tile_rows.transpose(1, 3, 5, 0, 2, 4, 6).reshape(N_GZ * N_GX, N_GY, NG, CELLS)
    weights = los_weight.reshape(N_GZ * N_GX, N_GY, KS, CELLS, PB)
    owners = slot_owner.reshape(N_GZ * N_GX, N_GY, KS).astype(jnp.int32)
    blocks = slot_block.reshape(N_GZ * N_GX, N_GY, KS).astype(jnp.int32)

    def project(operands):
        row_tiles, row_weights, row_owners, row_blocks = operands
        contrib = jnp.einsum("jgc,jscp->jsgp", row_tiles.astype(jnp.float32), row_weights.astype(jnp.float32), precision=lax.Precision.HIGHEST)
        target = (row_owners * BO + row_blocks).reshape(-1).astype(jnp.int32)
        return jax.ops.segment_sum(contrib.reshape(N_GY * KS, NG, PB), target, num_segments=N_GY * BO)

    sky = lax.map(project, (tile_rows, weights, owners, blocks))
    return density, sky.reshape(N_GZ, N_GX, N_GY * BO, NG, PB)
```

```python
import functools

import jax
import jax.numpy as jnp
from jax import lax
from jax.experimental import pallas as pl
from jax.experimental.pallas import tpu as pltpu
from jax.sharding import PartitionSpec as P

NE = 64
NG = 96
PB = 128
CX = 4
CZ = 4
CY = 128
KS = 7
BO = 4
CAP = 2
ZX = CZ * CX
LANE = CAP * NE + 8
VMEM = pl.BlockSpec(memory_space=pltpu.VMEM)
SMEM = pl.BlockSpec(memory_space=pltpu.SMEM)
SMALL = 16 * 1024 * 1024


def even(axis):
    return lax.rem(lax.axis_index(axis), 2) == 0


def lanes(shape=(NE, CY)):
    return lax.broadcasted_iota(jnp.int32, shape, 1)


def native(ref):
    return [ref[pl.ds(zx, NE, stride=ZX), :] for zx in range(ZX)]


def regrouped(ref):
    return [ref[zx * NE:(zx + 1) * NE, :] for zx in range(ZX)]


def put_faces(cells, outs):
    xa, xb, za, zb, ya, yb = outs
    px, py, pz = even("gx"), even("gy"), even("gz")
    for z in range(CZ):
        low, high = cells[z * CX], cells[z * CX + CX - 1]
        xa[z * NE:(z + 1) * NE, :] = jnp.where(px, high, low)
        xb[z * NE:(z + 1) * NE, :] = jnp.where(px, low, high)
    for x in range(CX):
        low, high = cells[x], cells[(CZ - 1) * CX + x]
        za[x * NE:(x + 1) * NE, :] = jnp.where(pz, high, low)
        zb[x * NE:(x + 1) * NE, :] = jnp.where(pz, low, high)
    lane = lanes()
    low = jnp.zeros((NE, CY), jnp.float32)
    high = jnp.zeros((NE, CY), jnp.float32)
    for zx in range(ZX):
        first = cells[zx] if zx == 0 else pltpu.roll(cells[zx], zx, 1)
        low = jnp.where(lane == zx, first, low)
        high = jnp.where(lane == zx, pltpu.roll(cells[zx], zx + 1, 1), high)
    ya[...] = jnp.where(py, high, low)
    yb[...] = jnp.where(py, low, high)


def column(row):
    square = jnp.broadcast_to(row, (NE, NE))
    across = lax.broadcasted_iota(jnp.int32, (NE, NE), 1)
    down = lax.broadcasted_iota(jnp.int32, (NE, NE), 0)
    return jnp.sum(jnp.where(across == down, square, 0.0), axis=1, keepdims=True)


def advance(cells, halos, diff_ref, loss_ref):
    xa, xb, za, zb, ya, yb = halos
    px, py, pz = even("gx"), even("gy"), even("gz")

    def sides(flag, a, b):
        return jnp.where(flag, b, a), jnp.where(flag, a, b)

    diff = jnp.broadcast_to(column(diff_ref[...]), (NE, CY))
    loss = jnp.broadcast_to(column(loss_ref[...]), (NE, CY))
    y_low, y_high = sides(py, ya[...], yb[...])
    lane = lanes()
    last = lax.broadcasted_iota(jnp.int32, (NE, CY), 0) == NE - 1
    out = []
    for z in range(CZ):
        x_low, x_high = sides(px, xa[z * NE:(z + 1) * NE, :], xb[z * NE:(z + 1) * NE, :])
        for x in range(CX):
            zx = z * CX + x
            c = cells[zx]
            if z in (0, CZ - 1):
                z_low, z_high = sides(pz, za[x * NE:(x + 1) * NE, :], zb[x * NE:(x + 1) * NE, :])
            z_up = cells[zx + CX] if z < CZ - 1 else z_high
            z_down = cells[zx - CX] if z > 0 else z_low
            x_up = cells[zx + 1] if x < CX - 1 else x_high
            x_down = cells[zx - 1] if x > 0 else x_low
            low = y_low if zx == 0 else pltpu.roll(y_low, CY - zx, 1)
            y_up = jnp.where(lane == CY - 1, pltpu.roll(y_high, CY - 1 - zx, 1), pltpu.roll(c, CY - 1, 1))
            y_down = jnp.where(lane == 0, low, pltpu.roll(c, 1, 1))
            beside = z_up + z_down + x_up + x_down + y_up + y_down
            flux = loss * c
            above = jnp.where(last, 0.0, pltpu.roll(flux, NE - 1, 0))
            out.append(c + diff * (beside - 6.0 * c) + above - flux)
    return out


def first_faces(cr_ref, *outs):
    put_faces(native(cr_ref), outs)


def middle_step(cr_ref, xa, xb, za, zb, ya, yb, diff_ref, loss_ref, next_ref, *outs):
    cells = advance(native(cr_ref), (xa, xb, za, zb, ya, yb), diff_ref, loss_ref)
    for zx in range(ZX):
        next_ref[zx * NE:(zx + 1) * NE, :] = cells[zx]
    put_faces(cells, outs)


def last_step(owner_ref, block_ref, now_ref, xa, xb, za, zb, ya, yb, diff_ref, loss_ref, gas_ref, weight_ref,
              final_ref, send_ref, parts_ref):
    cells = advance(regrouped(now_ref), (xa, xb, za, zb, ya, yb), diff_ref, loss_ref)
    for zx in range(ZX):
        final_ref[pl.ds(zx, NE, stride=ZX), :] = cells[zx]
        lit = cells[zx] * gas_ref[zx:zx + 1, :]
        upper = lit.astype(jnp.bfloat16)
        parts_ref[0:NE, zx * CY:(zx + 1) * CY] = upper
        parts_ref[NE:2 * NE, zx * CY:(zx + 1) * CY] = (lit - upper.astype(jnp.float32)).astype(jnp.bfloat16)
    send_ref[...] = jnp.zeros_like(send_ref)
    for s in range(KS):
        owner = owner_ref[s]
        place = 0
        for t in range(s):
            place = place + (owner_ref[t] == owner).astype(jnp.int32)
        product = jnp.dot(parts_ref[...], weight_ref[s], preferred_element_type=jnp.float32)
        base = owner * LANE
        at = pl.multiple_of(base + place * NE, 8)
        send_ref[pl.ds(at, NE), :] = product[:NE] + product[NE:]
        mark = base + CAP * NE + place * BO + block_ref[s]
        send_ref[pl.ds(mark, 1), :] = jnp.ones((1, PB), jnp.float32)


def gather_sky(recv_ref, table_ref, sky_ref):
    count = recv_ref.shape[0] // LANE
    total = [jnp.zeros((NE, PB), jnp.float32) for _ in range(BO)]
    for j in range(count):
        for k in range(CAP):
            block = recv_ref[j * LANE + k * NE:j * LANE + (k + 1) * NE, :]
            for b in range(BO):
                row = j * LANE + CAP * NE + k * BO + b
                total[b] = total[b] + block * recv_ref[row:row + 1, :]
    for b in range(BO):
        sky_ref[b * NG:(b + 1) * NG, :] = jnp.dot(
            table_ref[...], total[b], precision=lax.Precision.HIGHEST, preferred_element_type=jnp.float32
        )


def f32(*shape):
    return jax.ShapeDtypeStruct(shape, jnp.float32)


FACES = [f32(CZ * NE, CY)] * 2 + [f32(CX * NE, CY)] * 2 + [f32(NE, CY)] * 2


def call(body, name, outs, in_specs, scratch=()):
    return pl.pallas_call(
        body,
        name=name,
        out_shape=outs,
        in_specs=in_specs,
        out_specs=[VMEM] * len(outs),
        scratch_shapes=list(scratch),
        compiler_params=pltpu.CompilerParams(vmem_limit_bytes=SMALL),
    )


def swap(values, axis, start):
    pairs = []
    for i in range(start, lax.axis_size(axis) - 1, 2):
        pairs += [(i, i + 1), (i + 1, i)]
    return lax.ppermute(values, axis, pairs)


def exchange(faces):
    xa, xb, za, zb, ya, yb = faces
    far = swap(xb, "gx", 1)
    return (swap(xa, "gx", 0), far, swap(za, "gz", 0), swap(zb, "gz", 1), swap(ya, "gy", 0), swap(yb, "gy", 1))


def body(cr_init, gas, diff_coeff, loss_coeff, pi0_table, los_weight, slot_owner, slot_block):
    start = cr_init.reshape(NE * ZX, CY)
    diff, loss = diff_coeff.reshape(1, NE), loss_coeff.reshape(1, NE)
    faces = call(first_faces, "first_faces", FACES, [VMEM])(start)
    now, *faces = call(middle_step, "middle_step", [f32(ZX * NE, CY)] + FACES, [VMEM] * 9)(
        start, *exchange(faces), diff, loss
    )
    owners = lax.axis_size("gy")
    final, send = call(
        last_step,
        "last_step",
        [f32(NE * ZX, CY), f32(owners * LANE, PB)],
        [SMEM] * 2 + [VMEM] * 11,
        [pltpu.VMEM((2 * NE, ZX * CY), jnp.bfloat16)],
    )(
        slot_owner.reshape(KS), slot_block.reshape(KS), now, *exchange(faces), diff, loss,
        gas.reshape(ZX, CY), los_weight.reshape(KS, ZX * CY, PB),
    )
    recv = lax.all_to_all(send.reshape(owners, LANE, PB), "gy", 0, 0, tiled=True)
    (sky,) = call(gather_sky, "gather_sky", [f32(BO * NG, PB)], [VMEM] * 2)(
        recv.reshape(owners * LANE, PB), pi0_table
    )
    return final.reshape(cr_init.shape), sky.reshape(1, 1, BO, NG, PB)


def solution(mesh):
    in_specs = (
        P(None, "gz", "gx", "gy"),
        P("gz", "gx", "gy"),
        P(),
        P(),
        P(),
        P("gz", "gx", "gy", None, None, None),
        P("gz", "gx", "gy", None, None),
        P("gz", "gx", "gy", None),
    )
    out_specs = (P(None, "gz", "gx", "gy"), P("gz", "gx", "gy", None, None))
    return jax.shard_map(body, mesh=mesh, in_specs=in_specs, out_specs=out_specs, check_vma=False)
```

```python
import jax
import jax.numpy as jnp
from jax import lax
from jax.experimental import pallas as pl
from jax.experimental.pallas import tpu as pltpu
from jax.sharding import PartitionSpec as P

NE = 64
NG = 96
PB = 128
CX = 4
CZ = 4
CY = 128
KS = 7
BO = 4
CAP = 2
ZX = CZ * CX
LANE = CAP * NE + 8
VMEM = pl.BlockSpec(memory_space=pltpu.VMEM)
SMEM = pl.BlockSpec(memory_space=pltpu.SMEM)
HBM = pl.BlockSpec(memory_space=pltpu.MemorySpace.HBM)
SMALL = 16 * 1024 * 1024
LARGE = 50 * 1024 * 1024


def even(axis):
    return lax.rem(lax.axis_index(axis), 2) == 0


def tile(ref, row):
    return ref[row * NE:(row + 1) * NE, :]


def native(ref):
    return [ref[pl.ds(zx, NE, stride=ZX), :] for zx in range(ZX)]


def lanes():
    return lax.broadcasted_iota(jnp.int32, (NE, CY), 1)


def moved(values, shift):
    return values if shift % CY == 0 else pltpu.roll(values, shift % CY, 1)


def gather_columns(entries):
    lane = lanes()
    packed = jnp.zeros((NE, CY), jnp.float32)
    for to, values, at in entries:
        packed = jnp.where(lane == to, moved(values, to - at), packed)
    return packed


def first_faces(cr_ref, xa, xb, za, zb):
    cells = native(cr_ref)
    px, pz = even("gx"), even("gz")
    for depth in range(2):
        for i in range(4):
            row = (depth * 4 + i) * NE
            low, high = cells[i * CX + depth], cells[i * CX + CX - 1 - depth]
            xa[row:row + NE, :] = jnp.where(px, high, low)
            xb[row:row + NE, :] = jnp.where(px, low, high)
            low, high = cells[depth * CX + i], cells[(CZ - 1 - depth) * CX + i]
            za[row:row + NE, :] = jnp.where(pz, high, low)
            zb[row:row + NE, :] = jnp.where(pz, low, high)


def halo_rows(flag, a_ref, b_ref, count):
    pairs = [(tile(a_ref, i), tile(b_ref, i)) for i in range(count)]
    return [jnp.where(flag, b, a) for a, b in pairs], [jnp.where(flag, a, b) for a, b in pairs]


def edge_faces(cr_ref, xa, xb, za, zb, ya_out, yb_out, ea_out, eb_out):
    cells = native(cr_ref)
    px, py, pz = even("gx"), even("gy"), even("gz")
    x_low, x_high = halo_rows(px, xa, xb, CZ)
    z_low, z_high = halo_rows(pz, za, zb, CX)
    packs = []
    for near in (0, CY - 1):
        deep = 1 if near == 0 else CY - 2
        entries = []
        for zx in range(ZX):
            entries.append((zx, cells[zx], near))
            entries.append((ZX + zx, cells[zx], deep))
        for i in range(4):
            entries.append((2 * ZX + i * CX, x_low[i], near))
            entries.append((2 * ZX + i * CX + CX - 1, x_high[i], near))
            entries.append((3 * ZX + i, z_low[i], near))
            entries.append((3 * ZX + (CZ - 1) * CX + i, z_high[i], near))
        packs.append(gather_columns(entries))
    low, high = packs
    ya_out[...] = jnp.where(py, high, low)
    yb_out[...] = jnp.where(py, low, high)
    for i, rows in enumerate((x_low, x_high)):
        ea_out[i * NE:(i + 1) * NE, :] = jnp.where(pz, rows[CZ - 1], rows[0])
        eb_out[i * NE:(i + 1) * NE, :] = jnp.where(pz, rows[0], rows[CZ - 1])


def column(row):
    square = jnp.broadcast_to(row, (NE, NE))
    across = lax.broadcasted_iota(jnp.int32, (NE, NE), 1)
    down = lax.broadcasted_iota(jnp.int32, (NE, NE), 0)
    return jnp.sum(jnp.where(across == down, square, 0.0), axis=1, keepdims=True)


def two_steps(cr_ref, halos, diff_ref, loss_ref):
    xa, xb, za, zb, ya, yb, ea, eb = halos
    px, py, pz = even("gx"), even("gy"), even("gz")
    lane = lanes()
    top = lax.broadcasted_iota(jnp.int32, (NE, CY), 0) == NE - 1
    diff = jnp.broadcast_to(column(diff_ref[...]), (NE, CY))
    loss = jnp.broadcast_to(column(loss_ref[...]), (NE, CY))
    inside = {}
    for axis in ("gx", "gy", "gz"):
        at = lax.axis_index(axis)
        inside[axis] = (at > 0, at < lax.axis_size(axis) - 1)

    def update(c, z_up, z_down, x_up, x_down, y_up, y_down):
        beside = z_up + z_down + x_up + x_down + y_up + y_down
        flux = loss * c
        above = jnp.where(top, 0.0, pltpu.roll(flux, NE - 1, 0))
        return c + diff * (beside - 6.0 * c) + above - flux

    def beside_y(c, low, low_lane, high, high_lane):
        y_up = jnp.where(lane == CY - 1, moved(high, CY - 1 - high_lane), pltpu.roll(c, CY - 1, 1))
        y_down = jnp.where(lane == 0, moved(low, -low_lane), pltpu.roll(c, 1, 1))
        return y_up, y_down

    cells = native(cr_ref)
    x_low, x_high = halo_rows(px, xa, xb, 2 * CZ)
    z_low, z_high = halo_rows(pz, za, zb, 2 * CX)
    e_low, e_high = halo_rows(pz, ea, eb, 2)
    (y_low,), (y_high,) = halo_rows(py, ya, yb, 1)

    def at(z, x):
        if 0 <= z < CZ and 0 <= x < CX:
            return cells[z * CX + x]
        if 0 <= z < CZ:
            return x_low[(-1 - x) * CZ + z] if x < 0 else x_high[(x - CX) * CZ + z]
        if 0 <= x < CX:
            return z_low[(-1 - z) * CX + x] if z < 0 else z_high[(z - CZ) * CX + x]
        return (e_low if z < 0 else e_high)[0 if x < 0 else 1]

    def y_lane(z, x):
        if 0 <= z < CZ and 0 <= x < CX:
            return z * CX + x
        if 0 <= z < CZ:
            return 2 * ZX + z * CX + (0 if x < 0 else CX - 1)
        return 3 * ZX + (0 if z < 0 else (CZ - 1) * CX) + x

    def first(z, x):
        c, place = at(z, x), y_lane(z, x)
        new = update(c, at(z + 1, x), at(z - 1, x), at(z, x + 1), at(z, x - 1), *beside_y(c, y_low, place, y_high, place))
        if z in (-1, CZ):
            return jnp.where(inside["gz"][0 if z < 0 else 1], new, 0.0)
        if x in (-1, CX):
            return jnp.where(inside["gx"][0 if x < 0 else 1], new, 0.0)
        return new

    def first_y(pack, own, upper):
        cx, cz = lax.rem(lane, CX), lax.div(lane, CX)
        deep, x_edge, z_edge = moved(pack, -ZX), moved(pack, -2 * ZX), moved(pack, -3 * ZX)
        z_up = jnp.where(cz == CZ - 1, z_edge, moved(pack, -CX))
        z_down = jnp.where(cz == 0, z_edge, moved(pack, CX))
        x_up = jnp.where(cx == CX - 1, x_edge, moved(pack, -1))
        x_down = jnp.where(cx == 0, x_edge, moved(pack, 1))
        new = update(pack, z_up, z_down, x_up, x_down, *((deep, own) if upper else (own, deep)))
        return jnp.where(inside["gy"][1 if upper else 0], new, 0.0)

    own_low = gather_columns([(zx, cells[zx], 0) for zx in range(ZX)])
    own_high = gather_columns([(zx, cells[zx], CY - 1) for zx in range(ZX)])
    next_y_low = first_y(y_low, own_low, False)
    next_y_high = first_y(y_high, own_high, True)
    ring = [(z, x) for z in range(CZ) for x in (-1, CX)] + [(z, x) for z in (-1, CZ) for x in range(CX)]
    now = {zx: first(*zx) for zx in [(z, x) for z in range(CZ) for x in range(CX)] + ring}
    out = []
    for z in range(CZ):
        for x in range(CX):
            c, place = now[z, x], z * CX + x
            out.append(update(c, now[z + 1, x], now[z - 1, x], now[z, x + 1], now[z, x - 1],
                              *beside_y(c, next_y_low, place, next_y_high, place)))
    return out


def project(owner_ref, block_ref, cr_ref, xa, xb, za, zb, ya, yb, ea, eb, diff_ref, loss_ref, gas_ref, weight_hbm,
            final_ref, send_ref, parts_ref, weight_ref, sems):
    copies = [pltpu.make_async_copy(weight_hbm.at[s], weight_ref.at[s], sems.at[s]) for s in range(KS)]
    for copy in copies:
        copy.start()
    cells = two_steps(cr_ref, (xa, xb, za, zb, ya, yb, ea, eb), diff_ref, loss_ref)
    for zx in range(ZX):
        final_ref[pl.ds(zx, NE, stride=ZX), :] = cells[zx]
        lit = cells[zx] * gas_ref[zx:zx + 1, :]
        upper = lit.astype(jnp.bfloat16)
        parts_ref[0:NE, zx * CY:(zx + 1) * CY] = upper
        parts_ref[NE:2 * NE, zx * CY:(zx + 1) * CY] = (lit - upper.astype(jnp.float32)).astype(jnp.bfloat16)
    send_ref[...] = jnp.zeros_like(send_ref)
    for s in range(KS):
        owner = owner_ref[s]
        place = 0
        for t in range(s):
            place = place + (owner_ref[t] == owner).astype(jnp.int32)
        copies[s].wait()
        product = jnp.dot(parts_ref[...], weight_ref[s], preferred_element_type=jnp.float32)
        base = owner * LANE
        send_ref[pl.ds(pl.multiple_of(base + place * NE, 8), NE), :] = product[:NE] + product[NE:]
        mark = base + CAP * NE + place * BO + block_ref[s]
        send_ref[pl.ds(mark, 1), :] = jnp.ones((1, PB), jnp.float32)


def gather_sky(recv_ref, table_ref, sky_ref):
    count = recv_ref.shape[0] // LANE
    total = [jnp.zeros((NE, PB), jnp.float32) for _ in range(BO)]
    for j in range(count):
        for k in range(CAP):
            block = recv_ref[j * LANE + k * NE:j * LANE + (k + 1) * NE, :]
            for b in range(BO):
                row = j * LANE + CAP * NE + k * BO + b
                total[b] = total[b] + block * recv_ref[row:row + 1, :]
    for b in range(BO):
        sky_ref[b * NG:(b + 1) * NG, :] = jnp.dot(
            table_ref[...], total[b], precision=lax.Precision.HIGHEST, preferred_element_type=jnp.float32
        )


def f32(*shape):
    return jax.ShapeDtypeStruct(shape, jnp.float32)


def call(body, name, outs, in_specs, scratch=(), limit=SMALL):
    return pl.pallas_call(
        body,
        name=name,
        out_shape=outs,
        in_specs=in_specs,
        out_specs=[VMEM] * len(outs),
        scratch_shapes=list(scratch),
        compiler_params=pltpu.CompilerParams(vmem_limit_bytes=limit),
    )


def swap(values, axis, start):
    pairs = []
    for i in range(start, lax.axis_size(axis) - 1, 2):
        pairs += [(i, i + 1), (i + 1, i)]
    return lax.ppermute(values, axis, pairs)


def body(cr_init, gas, diff_coeff, loss_coeff, pi0_table, los_weight, slot_owner, slot_block):
    start = cr_init.reshape(NE * ZX, CY)
    diff, loss = diff_coeff.reshape(1, NE), loss_coeff.reshape(1, NE)
    xa, xb, za, zb = call(first_faces, "first_faces", [f32(2 * 4 * NE, CY)] * 4, [VMEM])(start)
    xb = swap(xb, "gx", 1)
    xa = swap(xa, "gx", 0)
    za = swap(za, "gz", 0)
    zb = swap(zb, "gz", 1)
    ya, yb, ea, eb = call(edge_faces, "edge_faces", [f32(NE, CY)] * 2 + [f32(2 * NE, CY)] * 2, [VMEM] * 5)(
        start, xa, xb, za, zb
    )
    yb = swap(yb, "gy", 1)
    ya = swap(ya, "gy", 0)
    ea = swap(ea, "gz", 0)
    eb = swap(eb, "gz", 1)
    owners = lax.axis_size("gy")
    final, send = call(
        project,
        "project",
        [f32(NE * ZX, CY), f32(owners * LANE, PB)],
        [SMEM] * 2 + [VMEM] * 12 + [HBM],
        [
            pltpu.VMEM((2 * NE, ZX * CY), jnp.bfloat16),
            pltpu.VMEM((KS, ZX * CY, PB), jnp.bfloat16),
            pltpu.SemaphoreType.DMA((KS,)),
        ],
        LARGE,
    )(
        slot_owner.reshape(KS), slot_block.reshape(KS), start, xa, xb, za, zb, ya, yb, ea, eb, diff, loss,
        gas.reshape(ZX, CY), los_weight.reshape(KS, ZX * CY, PB),
    )
    recv = lax.all_to_all(send.reshape(owners, LANE, PB), "gy", 0, 0, tiled=True)
    (sky,) = call(gather_sky, "gather_sky", [f32(BO * NG, PB)], [VMEM] * 2)(
        recv.reshape(owners * LANE, PB), pi0_table
    )
    return final.reshape(cr_init.shape), sky.reshape(1, 1, BO, NG, PB)


def solution(mesh):
    in_specs = (
        P(None, "gz", "gx", "gy"),
        P("gz", "gx", "gy"),
        P(),
        P(),
        P(),
        P("gz", "gx", "gy", None, None, None),
        P("gz", "gx", "gy", None, None),
        P("gz", "gx", "gy", None),
    )
    out_specs = (P(None, "gz", "gx", "gy"), P("gz", "gx", "gy", None, None))
    return jax.shard_map(body, mesh=mesh, in_specs=in_specs, out_specs=out_specs, check_vma=False)
```

```python
import jax
import jax.numpy as jnp
from jax import lax
from jax.experimental import pallas as pl
from jax.experimental.pallas import tpu as pltpu
from jax.sharding import PartitionSpec as P

NE = 64
NG = 96
PB = 128
CX = 4
CZ = 4
CY = 128
KS = 7
BO = 4
CAP = 2
ZX = CZ * CX
LANE = CAP * NE + 8
VMEM = pl.BlockSpec(memory_space=pltpu.VMEM)
ANY = pl.BlockSpec(memory_space=pl.ANY)
SMALL = 16 * 1024 * 1024


def even(axis):
    return lax.rem(lax.axis_index(axis), 2) == 0


def tile(ref, row):
    return ref[row * NE:(row + 1) * NE, :]


def native(ref):
    return [ref[pl.ds(zx, NE, stride=ZX), :] for zx in range(ZX)]


def lanes():
    return lax.broadcasted_iota(jnp.int32, (NE, CY), 1)


def moved(values, shift):
    return values if shift % CY == 0 else pltpu.roll(values, shift % CY, 1)


def gather_columns(packed, entries):
    lane = lanes()
    for to, values, at in entries:
        packed = jnp.where(lane == to, moved(values, to - at), packed)
    return packed


def first_faces(cr_ref, xa, xb, za, zb):
    cells = native(cr_ref)
    px, pz = even("gx"), even("gz")
    for depth in range(2):
        for i in range(4):
            row = (depth * 4 + i) * NE
            low, high = cells[i * CX + depth], cells[i * CX + CX - 1 - depth]
            xa[row:row + NE, :] = jnp.where(px, high, low)
            xb[row:row + NE, :] = jnp.where(px, low, high)
            low, high = cells[depth * CX + i], cells[(CZ - 1 - depth) * CX + i]
            za[row:row + NE, :] = jnp.where(pz, high, low)
            zb[row:row + NE, :] = jnp.where(pz, low, high)


def halo_rows(flag, a_ref, b_ref, count):
    pairs = [(tile(a_ref, i), tile(b_ref, i)) for i in range(count)]
    return [jnp.where(flag, b, a) for a, b in pairs], [jnp.where(flag, a, b) for a, b in pairs]


def place_of(owner_ref, s):
    place = 0
    for t in range(s):
        place = place + (owner_ref[t] == owner_ref[s]).astype(jnp.int32)
    return place


def blank_lanes(owner_any, block_any, send_ref, owner_ref, block_ref, sem):
    fetches = [
        pltpu.make_async_copy(owner_any, owner_ref, sem.at[0]), pltpu.make_async_copy(block_any, block_ref, sem.at[1])
    ]
    for fetch in fetches:
        fetch.start()
    send_ref[...] = jnp.zeros_like(send_ref)
    for fetch in fetches:
        fetch.wait()
    for s in range(KS):
        row = owner_ref[s] * LANE + CAP * NE + place_of(owner_ref, s) * BO + block_ref[s]
        send_ref[pl.ds(row, 1), :] = jnp.ones((1, PB), jnp.float32)


def own_columns(cr_ref, blank_any, low_ref, high_ref):
    del blank_any
    cells = native(cr_ref)
    for ref, near, deep in ((low_ref, 0, 1), (high_ref, CY - 1, CY - 2)):
        entries = [(4 * zx, cells[zx], near) for zx in range(ZX)] + [(4 * zx + 1, cells[zx], deep) for zx in range(ZX)]
        ref[...] = gather_columns(jnp.zeros((NE, CY), jnp.float32), entries)


def edge_faces(xa, xb, za, zb, low_ref, high_ref, ya_out, yb_out, ea_out, eb_out):
    px, py, pz = even("gx"), even("gy"), even("gz")
    x_low, x_high = halo_rows(px, xa, xb, CZ)
    z_low, z_high = halo_rows(pz, za, zb, CX)
    packs = []
    for ref, near in ((low_ref, 0), (high_ref, CY - 1)):
        entries = []
        for i in range(4):
            entries.append((4 * (i * CX) + 2, x_low[i], near))
            entries.append((4 * (i * CX + CX - 1) + 2, x_high[i], near))
            entries.append((4 * i + 3, z_low[i], near))
            entries.append((4 * ((CZ - 1) * CX + i) + 3, z_high[i], near))
        packs.append(gather_columns(ref[...], entries))
    low, high = packs
    ya_out[...] = jnp.where(py, high, low)
    yb_out[...] = jnp.where(py, low, high)
    for i, rows in enumerate((x_low, x_high)):
        ea_out[i * NE:(i + 1) * NE, :] = jnp.where(pz, rows[CZ - 1], rows[0])
        eb_out[i * NE:(i + 1) * NE, :] = jnp.where(pz, rows[0], rows[CZ - 1])


def column(row):
    square = jnp.broadcast_to(row, (NE, NE))
    across = lax.broadcasted_iota(jnp.int32, (NE, NE), 1)
    down = lax.broadcasted_iota(jnp.int32, (NE, NE), 0)
    return jnp.sum(jnp.where(across == down, square, 0.0), axis=1, keepdims=True)


def coefficients(diff_ref, loss_ref):
    return [jnp.broadcast_to(column(ref[...]), (NE, CY)) for ref in (diff_ref, loss_ref)]


def inside(axis):
    at = lax.axis_index(axis)
    return at > 0, at < lax.axis_size(axis) - 1


def stepper(diff, loss):
    top = lax.broadcasted_iota(jnp.int32, (NE, CY), 0) == NE - 1

    def update(c, beside):
        flux = loss * c
        above = jnp.where(top, 0.0, pltpu.roll(flux, NE - 1, 0))
        return c + diff * (beside - 6.0 * c) + above - flux

    return update


def inner_steps(cr_ref, xa, xb, za, zb, diff_ref, loss_ref, inner_ref):
    px, pz = even("gx"), even("gz")
    lane = lanes()
    diff, loss = coefficients(diff_ref, loss_ref)
    update = stepper(diff, loss)
    cells = native(cr_ref)
    x_low, x_high = halo_rows(px, xa, xb, 2 * CZ)
    z_low, z_high = halo_rows(pz, za, zb, 2 * CX)

    def along_y(c):
        return jnp.where(lane == CY - 1, 0.0, pltpu.roll(c, CY - 1, 1)) + jnp.where(lane == 0, 0.0, pltpu.roll(c, 1, 1))

    def at(z, x):
        if 0 <= z < CZ and 0 <= x < CX:
            return cells[z * CX + x]
        if 0 <= z < CZ:
            return x_low[(-1 - x) * CZ + z] if x < 0 else x_high[(x - CX) * CZ + z]
        if 0 <= x < CX:
            return z_low[(-1 - z) * CX + x] if z < 0 else z_high[(z - CZ) * CX + x]
        return None

    def around(get, z, x):
        found = [get(z + 1, x), get(z - 1, x), get(z, x + 1), get(z, x - 1)]
        found = [values for values in found if values is not None]
        return sum(found[1:], found[0])

    now = {}
    for z in range(-1, CZ + 1):
        for x in range(-1, CX + 1):
            if at(z, x) is None:
                continue
            new = around(at, z, x)
            if 0 <= z < CZ and 0 <= x < CX:
                now[z, x] = update(at(z, x), new + along_y(at(z, x)))
            else:
                axis, upper = ("gx", x > 0) if 0 <= z < CZ else ("gz", z > 0)
                now[z, x] = jnp.where(inside(axis)[1 if upper else 0], update(at(z, x), new), 0.0)
    for z in range(CZ):
        for x in range(CX):
            c = now[z, x]
            halos = [at(*there) for there in ((z + 1, x), (z - 1, x), (z, x + 1), (z, x - 1))
                     if not (0 <= there[0] < CZ and 0 <= there[1] < CX)]
            mixed = c + diff * sum(halos[1:], halos[0]) if halos else c
            row = (z * CX + x) * NE
            inner_ref[row:row + NE, :] = update(c, around(lambda *there: now[there], z, x) + along_y(mixed))


def y_corrections(pack, own, diff, loss, update, here):
    place = lax.div(lanes(), 4)
    cx, cz = lax.rem(place, CX), lax.div(place, CX)
    deep, x_edge, z_edge = moved(pack, -1), moved(pack, -2), moved(pack, -3)

    def around(values, x_halo, z_halo):
        return (
            jnp.where(cz == CZ - 1, z_halo, moved(values, -4 * CX)) + jnp.where(cz == 0, z_halo, moved(values, 4 * CX))
            + jnp.where(cx == CX - 1, x_halo, moved(values, -4)) + jnp.where(cx == 0, x_halo, moved(values, 4))
        )

    beyond = jnp.where(here, update(pack, around(pack, x_edge, z_edge) + deep + own), 0.0)
    first = diff * pack
    outer = update(first, around(first, diff * x_edge, diff * z_edge) + beyond)
    return outer, diff * first


def project(owner_any, lanes_any, inner_ref, low_ref, high_ref, ya, yb, ea, eb, diff_ref, loss_ref, gas_ref, weight_ref,
            cells_ref, send_any, parts_ref, blocks_ref, owner_ref, sem, owner_sem):
    del lanes_any
    fetch = pltpu.make_async_copy(owner_any, owner_ref, owner_sem)
    fetch.start()
    py, pz = even("gy"), even("gz")
    lane = lanes()
    diff, loss = coefficients(diff_ref, loss_ref)
    update = stepper(diff, loss)
    e_low, e_high = halo_rows(pz, ea, eb, 2)
    (y_low,), (y_high,) = halo_rows(py, ya, yb, 1)
    below, beyond = inside("gy")
    outer_low, next_low = y_corrections(y_low, low_ref[...], diff, loss, update, below)
    outer_high, next_high = y_corrections(y_high, high_ref[...], diff, loss, update, beyond)
    kind = lax.rem(lane, 4)
    mixed = jnp.where(kind == 0, outer_low, moved(next_low, 1))
    mixed = jnp.where(kind == 3, moved(outer_high, -1), mixed)
    mixed = jnp.where(kind == 2, moved(next_high, -2), mixed)
    rim = (lane < 2) | (lane >= CY - 2)
    corners = {0: e_low[0], CX - 1: e_low[1], (CZ - 1) * CX: e_high[0], ZX - 1: e_high[1]}
    for zx in range(ZX):
        cell = tile(inner_ref, zx) + jnp.where(rim, moved(mixed, -4 * zx), 0.0)
        if zx in corners:
            cell = cell + 2.0 * diff * diff * corners[zx]
        cells_ref[zx * NE:(zx + 1) * NE, :] = cell
        lit = cell * gas_ref[zx:zx + 1, :]
        upper = lit.astype(jnp.bfloat16)
        parts_ref[0:NE, zx * CY:(zx + 1) * CY] = upper
        parts_ref[NE:2 * NE, zx * CY:(zx + 1) * CY] = (lit - upper.astype(jnp.float32)).astype(jnp.bfloat16)
    weights = jnp.concatenate([weight_ref[s] for s in range(KS)], axis=1)
    product = jnp.dot(parts_ref[...], weights, preferred_element_type=jnp.float32)
    product = product[:NE] + product[NE:]
    for s in range(KS):
        blocks_ref[s * NE:(s + 1) * NE, :] = product[:, s * PB:(s + 1) * PB]
    fetch.wait()
    copies = []
    for s in range(KS):
        row = pl.multiple_of(owner_ref[s] * LANE + place_of(owner_ref, s) * NE, 8)
        copies.append(pltpu.make_async_copy(blocks_ref.at[pl.ds(s * NE, NE)], send_any.at[pl.ds(row, NE)], sem.at[s]))
        copies[s].start()
    for copy in copies:
        copy.wait()


def finish_density(cells_ref, final_ref):
    for zx in range(ZX):
        final_ref[pl.ds(zx, NE, stride=ZX), :] = tile(cells_ref, zx)


def gather_sky(recv_ref, table_ref, sky_ref):
    count = recv_ref.shape[0] // LANE
    total = [jnp.zeros((NE, PB), jnp.float32) for _ in range(BO)]
    for j in range(count):
        for k in range(CAP):
            block = recv_ref[j * LANE + k * NE:j * LANE + (k + 1) * NE, :]
            for b in range(BO):
                row = j * LANE + CAP * NE + k * BO + b
                total[b] = total[b] + block * recv_ref[row:row + 1, :]
    for b in range(BO):
        sky_ref[b * NG:(b + 1) * NG, :] = jnp.dot(
            table_ref[...], total[b], precision=lax.Precision.HIGHEST, preferred_element_type=jnp.float32
        )


def f32(*shape):
    return jax.ShapeDtypeStruct(shape, jnp.float32)


def cost(us):
    return pl.CostEstimate(flops=0, transcendentals=0, bytes_accessed=us * 3000000)


def call(body, name, outs, in_specs, us, out_specs=None, scratch=(), aliases=None):
    return pl.pallas_call(
        body,
        name=name,
        out_shape=outs,
        in_specs=in_specs,
        out_specs=out_specs or [VMEM] * len(outs),
        scratch_shapes=list(scratch),
        input_output_aliases=aliases or {},
        cost_estimate=cost(us),
        compiler_params=pltpu.CompilerParams(vmem_limit_bytes=SMALL),
    )


def swap(values, axis, start):
    pairs = []
    for i in range(start, lax.axis_size(axis) - 1, 2):
        pairs += [(i, i + 1), (i + 1, i)]
    return lax.ppermute(values, axis, pairs)


def body(cr_init, gas, diff_coeff, loss_coeff, pi0_table, los_weight, slot_owner, slot_block):
    start = cr_init.reshape(NE * ZX, CY)
    diff, loss = diff_coeff.reshape(1, NE), loss_coeff.reshape(1, NE)
    column_pack, edge_rows = f32(NE, CY), f32(2 * NE, CY)
    xa, xb, za, zb = call(first_faces, "first_faces", [f32(2 * 4 * NE, CY)] * 4, [VMEM], 1)(start)
    xb = swap(xb, "gx", 1)
    xa = swap(xa, "gx", 0)
    za = swap(za, "gz", 0)
    zb = swap(zb, "gz", 1)
    owner, owners = slot_owner.reshape(KS), lax.axis_size("gy")
    (blank,) = call(
        blank_lanes,
        "blank_lanes",
        [f32(owners * LANE, PB)],
        [ANY] * 2,
        1,
        scratch=[pltpu.SMEM((KS,), jnp.int32), pltpu.SMEM((KS,), jnp.int32), pltpu.SemaphoreType.DMA((2,))],
    )(owner, slot_block.reshape(KS))
    low, high = call(own_columns, "own_columns", [column_pack] * 2, [VMEM, ANY], 1)(start, blank)
    ya, yb, ea, eb = call(edge_faces, "edge_faces", [column_pack] * 2 + [edge_rows] * 2, [VMEM] * 6, 1)(
        xa, xb, za, zb, low, high
    )
    yb = swap(yb, "gy", 1)
    ya = swap(ya, "gy", 0)
    ea = swap(ea, "gz", 0)
    eb = swap(eb, "gz", 1)
    (inner,) = call(inner_steps, "inner_steps", [f32(ZX * NE, CY)], [VMEM] * 7, 2)(start, xa, xb, za, zb, diff, loss)
    cells, send = call(
        project,
        "project",
        [f32(ZX * NE, CY), f32(owners * LANE, PB)],
        [ANY] * 2 + [VMEM] * 11,
        2,
        out_specs=[VMEM, ANY],
        scratch=[
            pltpu.VMEM((2 * NE, ZX * CY), jnp.bfloat16),
            pltpu.VMEM((KS * NE, PB), jnp.float32),
            pltpu.SMEM((KS,), jnp.int32),
            pltpu.SemaphoreType.DMA((KS,)),
            pltpu.SemaphoreType.DMA,
        ],
        aliases={1: 1},
    )(
        owner, blank, inner, low, high, ya, yb, ea, eb, diff, loss,
        gas.reshape(ZX, CY), los_weight.reshape(KS, ZX * CY, PB),
    )
    (final,) = call(finish_density, "finish_density", [f32(NE * ZX, CY)], [VMEM], 2)(cells)
    recv = lax.all_to_all(send.reshape(owners, LANE, PB), "gy", 0, 0, tiled=True)
    (sky,) = call(gather_sky, "gather_sky", [f32(BO * NG, PB)], [VMEM] * 2, 1)(
        recv.reshape(owners * LANE, PB), pi0_table
    )
    return final.reshape(cr_init.shape), sky.reshape(1, 1, BO, NG, PB)


def solution(mesh):
    in_specs = (
        P(None, "gz", "gx", "gy"),
        P("gz", "gx", "gy"),
        P(),
        P(),
        P(),
        P("gz", "gx", "gy", None, None, None),
        P("gz", "gx", "gy", None, None),
        P("gz", "gx", "gy", None),
    )
    out_specs = (P(None, "gz", "gx", "gy"), P("gz", "gx", "gy", None, None))
    return jax.shard_map(body, mesh=mesh, in_specs=in_specs, out_specs=out_specs, check_vma=False)
```

```python
import jax
import jax.numpy as jnp
from jax import lax
from jax.experimental import pallas as pl
from jax.experimental.pallas import tpu as pltpu
from jax.sharding import PartitionSpec as P

NE = 64
NG = 96
PB = 128
CX = 4
CZ = 4
CY = 128
KS = 7
BO = 4
CAP = 2
ZX = CZ * CX
LANE = CAP * NE + 8
VMEM = pl.BlockSpec(memory_space=pltpu.VMEM)
ANY = pl.BlockSpec(memory_space=pl.ANY)
SMALL = 16 * 1024 * 1024


def even(axis):
    return lax.rem(lax.axis_index(axis), 2) == 0


def tile(ref, row):
    return ref[row * NE:(row + 1) * NE, :]


def native(ref):
    return [ref[pl.ds(zx, NE, stride=ZX), :] for zx in range(ZX)]


def lanes():
    return lax.broadcasted_iota(jnp.int32, (NE, CY), 1)


def moved(values, shift):
    return values if shift % CY == 0 else pltpu.roll(values, shift % CY, 1)


def gather_columns(packed, entries):
    lane = lanes()
    for to, values, at in entries:
        packed = jnp.where(lane == to, moved(values, to - at), packed)
    return packed


def first_faces(cr_ref, xa, xb, za, zb):
    cells = native(cr_ref)
    px, pz = even("gx"), even("gz")
    for depth in range(2):
        for i in range(4):
            row = (depth * 4 + i) * NE
            low, high = cells[i * CX + depth], cells[i * CX + CX - 1 - depth]
            xa[row:row + NE, :] = jnp.where(px, high, low)
            xb[row:row + NE, :] = jnp.where(px, low, high)
            low, high = cells[depth * CX + i], cells[(CZ - 1 - depth) * CX + i]
            za[row:row + NE, :] = jnp.where(pz, high, low)
            zb[row:row + NE, :] = jnp.where(pz, low, high)


def halo_rows(flag, a_ref, b_ref, count):
    pairs = [(tile(a_ref, i), tile(b_ref, i)) for i in range(count)]
    return [jnp.where(flag, b, a) for a, b in pairs], [jnp.where(flag, a, b) for a, b in pairs]


def place_of(owner_ref, s):
    place = 0
    for t in range(s):
        place = place + (owner_ref[t] == owner_ref[s]).astype(jnp.int32)
    return place


def blank_lanes(owner_any, block_any, send_ref, owner_ref, block_ref, sem):
    fetches = [
        pltpu.make_async_copy(owner_any, owner_ref, sem.at[0]), pltpu.make_async_copy(block_any, block_ref, sem.at[1])
    ]
    for fetch in fetches:
        fetch.start()
    send_ref[...] = jnp.zeros_like(send_ref)
    for fetch in fetches:
        fetch.wait()
    for s in range(KS):
        row = owner_ref[s] * LANE + CAP * NE + place_of(owner_ref, s) * BO + block_ref[s]
        send_ref[pl.ds(row, 1), :] = jnp.ones((1, PB), jnp.float32)


def own_columns(cr_ref, blank_any, low_ref, high_ref):
    del blank_any
    cells = native(cr_ref)
    for ref, near, deep in ((low_ref, 0, 1), (high_ref, CY - 1, CY - 2)):
        entries = [(4 * zx, cells[zx], near) for zx in range(ZX)] + [(4 * zx + 1, cells[zx], deep) for zx in range(ZX)]
        ref[...] = gather_columns(jnp.zeros((NE, CY), jnp.float32), entries)


def edge_faces(xa, xb, za, zb, low_ref, high_ref, ya_out, yb_out, ea_out, eb_out):
    px, py, pz = even("gx"), even("gy"), even("gz")
    x_low, x_high = halo_rows(px, xa, xb, CZ)
    z_low, z_high = halo_rows(pz, za, zb, CX)
    packs = []
    for ref, near in ((low_ref, 0), (high_ref, CY - 1)):
        entries = []
        for i in range(4):
            entries.append((4 * (i * CX) + 2, x_low[i], near))
            entries.append((4 * (i * CX + CX - 1) + 2, x_high[i], near))
            entries.append((4 * i + 3, z_low[i], near))
            entries.append((4 * ((CZ - 1) * CX + i) + 3, z_high[i], near))
        packs.append(gather_columns(ref[...], entries))
    low, high = packs
    ya_out[0:NE, :] = jnp.where(py, high, low)
    yb_out[0:NE, :] = jnp.where(py, low, high)
    for ref in (ya_out, yb_out):
        ref[NE:2 * NE, :] = jnp.zeros((NE, CY), jnp.float32)
    for i, rows in enumerate((x_low, x_high)):
        ea_out[i * NE:(i + 1) * NE, :] = jnp.where(pz, rows[CZ - 1], rows[0])
        eb_out[i * NE:(i + 1) * NE, :] = jnp.where(pz, rows[0], rows[CZ - 1])


def column(row):
    square = jnp.broadcast_to(row, (NE, NE))
    across = lax.broadcasted_iota(jnp.int32, (NE, NE), 1)
    down = lax.broadcasted_iota(jnp.int32, (NE, NE), 0)
    return jnp.sum(jnp.where(across == down, square, 0.0), axis=1, keepdims=True)


def coefficients(diff_ref, loss_ref):
    return [jnp.broadcast_to(column(ref[...]), (NE, CY)) for ref in (diff_ref, loss_ref)]


def inside(axis):
    at = lax.axis_index(axis)
    return at > 0, at < lax.axis_size(axis) - 1


def stepper(diff, loss):
    top = lax.broadcasted_iota(jnp.int32, (NE, CY), 0) == NE - 1

    def update(c, beside):
        flux = loss * c
        above = jnp.where(top, 0.0, pltpu.roll(flux, NE - 1, 0))
        return c + diff * (beside - 6.0 * c) + above - flux

    return update


def inner_steps(cr_ref, xa, xb, za, zb, diff_ref, loss_ref, inner_ref):
    px, pz = even("gx"), even("gz")
    lane = lanes()
    diff, loss = coefficients(diff_ref, loss_ref)
    update = stepper(diff, loss)
    cells = native(cr_ref)
    x_low, x_high = halo_rows(px, xa, xb, 2 * CZ)
    z_low, z_high = halo_rows(pz, za, zb, 2 * CX)

    def along_y(c):
        return jnp.where(lane == CY - 1, 0.0, pltpu.roll(c, CY - 1, 1)) + jnp.where(lane == 0, 0.0, pltpu.roll(c, 1, 1))

    def at(z, x):
        if 0 <= z < CZ and 0 <= x < CX:
            return cells[z * CX + x]
        if 0 <= z < CZ:
            return x_low[(-1 - x) * CZ + z] if x < 0 else x_high[(x - CX) * CZ + z]
        if 0 <= x < CX:
            return z_low[(-1 - z) * CX + x] if z < 0 else z_high[(z - CZ) * CX + x]
        return None

    def around(get, z, x):
        found = [get(z + 1, x), get(z - 1, x), get(z, x + 1), get(z, x - 1)]
        found = [values for values in found if values is not None]
        return sum(found[1:], found[0])

    now = {}
    for z in range(-1, CZ + 1):
        for x in range(-1, CX + 1):
            if at(z, x) is None:
                continue
            new = around(at, z, x)
            if 0 <= z < CZ and 0 <= x < CX:
                now[z, x] = update(at(z, x), new + along_y(at(z, x)))
            else:
                axis, upper = ("gx", x > 0) if 0 <= z < CZ else ("gz", z > 0)
                now[z, x] = jnp.where(inside(axis)[1 if upper else 0], update(at(z, x), new), 0.0)
    for z in range(CZ):
        for x in range(CX):
            c = now[z, x]
            halos = [at(*there) for there in ((z + 1, x), (z - 1, x), (z, x + 1), (z, x - 1))
                     if not (0 <= there[0] < CZ and 0 <= there[1] < CX)]
            mixed = c + diff * sum(halos[1:], halos[0]) if halos else c
            row = (z * CX + x) * NE
            inner_ref[row:row + NE, :] = update(c, around(lambda *there: now[there], z, x) + along_y(mixed))


def y_corrections(pack, own, diff, loss, update, here):
    place = lax.div(lanes(), 4)
    cx, cz = lax.rem(place, CX), lax.div(place, CX)
    deep, x_edge, z_edge = moved(pack, -1), moved(pack, -2), moved(pack, -3)

    def around(values, x_halo, z_halo):
        return (
            jnp.where(cz == CZ - 1, z_halo, moved(values, -4 * CX)) + jnp.where(cz == 0, z_halo, moved(values, 4 * CX))
            + jnp.where(cx == CX - 1, x_halo, moved(values, -4)) + jnp.where(cx == 0, x_halo, moved(values, 4))
        )

    beyond = jnp.where(here, update(pack, around(pack, x_edge, z_edge) + deep + own), 0.0)
    first = diff * pack
    outer = update(first, around(first, diff * x_edge, diff * z_edge) + beyond)
    return outer, diff * first


def project(owner_any, lanes_any, inner_ref, low_ref, high_ref, ya, yb, ea, eb, diff_ref, loss_ref, gas_ref, weight_ref,
            cells_ref, send_any, parts_ref, blocks_ref, owner_ref, sem, owner_sem):
    del lanes_any
    fetch = pltpu.make_async_copy(owner_any, owner_ref, owner_sem)
    fetch.start()
    py, pz = even("gy"), even("gz")
    lane = lanes()
    diff, loss = coefficients(diff_ref, loss_ref)
    update = stepper(diff, loss)
    e_low, e_high = halo_rows(pz, ea, eb, 2)
    (y_low,), (y_high,) = halo_rows(py, ya, yb, 1)
    below, beyond = inside("gy")
    outer_low, next_low = y_corrections(y_low, low_ref[...], diff, loss, update, below)
    outer_high, next_high = y_corrections(y_high, high_ref[...], diff, loss, update, beyond)
    kind = lax.rem(lane, 4)
    mixed = jnp.where(kind == 0, outer_low, moved(next_low, 1))
    mixed = jnp.where(kind == 3, moved(outer_high, -1), mixed)
    mixed = jnp.where(kind == 2, moved(next_high, -2), mixed)
    rim = (lane < 2) | (lane >= CY - 2)
    corners = {0: e_low[0], CX - 1: e_low[1], (CZ - 1) * CX: e_high[0], ZX - 1: e_high[1]}
    for zx in range(ZX):
        cell = tile(inner_ref, zx) + jnp.where(rim, moved(mixed, -4 * zx), 0.0)
        if zx in corners:
            cell = cell + 2.0 * diff * diff * corners[zx]
        cells_ref[zx * NE:(zx + 1) * NE, :] = cell
        lit = cell * gas_ref[zx:zx + 1, :]
        upper = lit.astype(jnp.bfloat16)
        parts_ref[0:NE, zx * CY:(zx + 1) * CY] = upper
        parts_ref[NE:2 * NE, zx * CY:(zx + 1) * CY] = (lit - upper.astype(jnp.float32)).astype(jnp.bfloat16)
    weights = jnp.concatenate([weight_ref[s] for s in range(KS)], axis=1)
    product = jnp.dot(parts_ref[...], weights, preferred_element_type=jnp.float32)
    product = product[:NE] + product[NE:]
    for s in range(KS):
        blocks_ref[s * NE:(s + 1) * NE, :] = product[:, s * PB:(s + 1) * PB]
    fetch.wait()
    copies = []
    for s in range(KS):
        row = pl.multiple_of(owner_ref[s] * LANE + place_of(owner_ref, s) * NE, 8)
        copies.append(pltpu.make_async_copy(blocks_ref.at[pl.ds(s * NE, NE)], send_any.at[pl.ds(row, NE)], sem.at[s]))
        copies[s].start()
    for copy in copies:
        copy.wait()


def finish_density(cells_ref, final_ref):
    for zx in range(ZX):
        final_ref[pl.ds(zx, NE, stride=ZX), :] = tile(cells_ref, zx)


def gather_sky(recv_ref, table_ref, sky_ref):
    count = recv_ref.shape[0] // LANE
    total = [jnp.zeros((NE, PB), jnp.float32) for _ in range(BO)]
    for j in range(count):
        for k in range(CAP):
            block = recv_ref[j * LANE + k * NE:j * LANE + (k + 1) * NE, :]
            for b in range(BO):
                row = j * LANE + CAP * NE + k * BO + b
                total[b] = total[b] + block * recv_ref[row:row + 1, :]
    for b in range(BO):
        sky_ref[b * NG:(b + 1) * NG, :] = jnp.dot(
            table_ref[...], total[b], precision=lax.Precision.HIGHEST, preferred_element_type=jnp.float32
        )


def f32(*shape):
    return jax.ShapeDtypeStruct(shape, jnp.float32)


def cost(us):
    return pl.CostEstimate(flops=0, transcendentals=0, bytes_accessed=us * 3000000)


def call(body, name, outs, in_specs, us, out_specs=None, scratch=(), aliases=None):
    return pl.pallas_call(
        body,
        name=name,
        out_shape=outs,
        in_specs=in_specs,
        out_specs=out_specs or [VMEM] * len(outs),
        scratch_shapes=list(scratch),
        input_output_aliases=aliases or {},
        cost_estimate=cost(us),
        compiler_params=pltpu.CompilerParams(vmem_limit_bytes=SMALL),
    )


def swap(values, axis, start):
    pairs = []
    for i in range(start, lax.axis_size(axis) - 1, 2):
        pairs += [(i, i + 1), (i + 1, i)]
    return lax.ppermute(values, axis, pairs)


def body(cr_init, gas, diff_coeff, loss_coeff, pi0_table, los_weight, slot_owner, slot_block):
    start = cr_init.reshape(NE * ZX, CY)
    diff, loss = diff_coeff.reshape(1, NE), loss_coeff.reshape(1, NE)
    column_pack, edge_rows = f32(NE, CY), f32(2 * NE, CY)
    xa, xb, za, zb = call(first_faces, "first_faces", [f32(2 * 4 * NE, CY)] * 4, [VMEM], 1)(start)
    xb = swap(xb, "gx", 1)
    xa = swap(xa, "gx", 0)
    za = swap(za, "gz", 0)
    zb = swap(zb, "gz", 1)
    owner, owners = slot_owner.reshape(KS), lax.axis_size("gy")
    (blank,) = call(
        blank_lanes,
        "blank_lanes",
        [f32(owners * LANE, PB)],
        [ANY] * 2,
        1,
        scratch=[pltpu.SMEM((KS,), jnp.int32), pltpu.SMEM((KS,), jnp.int32), pltpu.SemaphoreType.DMA((2,))],
    )(owner, slot_block.reshape(KS))
    low, high = call(own_columns, "own_columns", [column_pack] * 2, [VMEM, ANY], 1)(start, blank)
    ya, yb, ea, eb = call(edge_faces, "edge_faces", [edge_rows] * 4, [VMEM] * 6, 1)(
        xa, xb, za, zb, low, high
    )
    yb = swap(yb, "gy", 1)
    ya = swap(ya, "gy", 0)
    ea = swap(ea, "gz", 0)
    eb = swap(eb, "gz", 1)
    (inner,) = call(inner_steps, "inner_steps", [f32(ZX * NE, CY)], [VMEM] * 7, 2)(start, xa, xb, za, zb, diff, loss)
    cells, send = call(
        project,
        "project",
        [f32(ZX * NE, CY), f32(owners * LANE, PB)],
        [ANY] * 2 + [VMEM] * 11,
        2,
        out_specs=[VMEM, ANY],
        scratch=[
            pltpu.VMEM((2 * NE, ZX * CY), jnp.bfloat16),
            pltpu.VMEM((KS * NE, PB), jnp.float32),
            pltpu.SMEM((KS,), jnp.int32),
            pltpu.SemaphoreType.DMA((KS,)),
            pltpu.SemaphoreType.DMA,
        ],
        aliases={1: 1},
    )(
        owner, blank, inner, low, high, ya, yb, ea, eb, diff, loss,
        gas.reshape(ZX, CY), los_weight.reshape(KS, ZX * CY, PB),
    )
    (final,) = call(finish_density, "finish_density", [f32(NE * ZX, CY)], [VMEM], 2)(cells)
    recv = lax.all_to_all(send.reshape(owners, LANE, PB), "gy", 0, 0, tiled=True)
    (sky,) = call(gather_sky, "gather_sky", [f32(BO * NG, PB)], [VMEM] * 2, 1)(
        recv.reshape(owners * LANE, PB), pi0_table
    )
    return final.reshape(cr_init.shape), sky.reshape(1, 1, BO, NG, PB)


def solution(mesh):
    in_specs = (
        P(None, "gz", "gx", "gy"),
        P("gz", "gx", "gy"),
        P(),
        P(),
        P(),
        P("gz", "gx", "gy", None, None, None),
        P("gz", "gx", "gy", None, None),
        P("gz", "gx", "gy", None),
    )
    out_specs = (P(None, "gz", "gx", "gy"), P("gz", "gx", "gy", None, None))
    return jax.shard_map(body, mesh=mesh, in_specs=in_specs, out_specs=out_specs, check_vma=False)
```

```python
import jax
import jax.numpy as jnp
from jax import lax
from jax.experimental import pallas as pl
from jax.experimental.pallas import tpu as pltpu
from jax.sharding import PartitionSpec as P

NE = 64
NG = 96
PB = 128
CX = 4
CZ = 4
CY = 128
KS = 7
BO = 4
CAP = 2
ZX = CZ * CX
LANE = CAP * NE + 1
VMEM = pl.BlockSpec(memory_space=pltpu.VMEM)
ANY = pl.BlockSpec(memory_space=pl.ANY)
SMALL = 16 * 1024 * 1024


def even(axis):
    return lax.rem(lax.axis_index(axis), 2) == 0


def tile(ref, row):
    return ref[row * NE:(row + 1) * NE, :]


def native(ref):
    return [ref[pl.ds(zx, NE, stride=ZX), :] for zx in range(ZX)]


def lanes():
    return lax.broadcasted_iota(jnp.int32, (NE, CY), 1)


def moved(values, shift):
    return values if shift % CY == 0 else pltpu.roll(values, shift % CY, 1)


def gather_columns(packed, entries):
    lane = lanes()
    for to, values, at in entries:
        packed = jnp.where(lane == to, moved(values, to - at), packed)
    return packed


def first_faces(cr_ref, xa, xb, za, zb):
    cells = native(cr_ref)
    px, pz = even("gx"), even("gz")
    for depth in range(2):
        for i in range(4):
            row = (depth * 4 + i) * NE
            low, high = cells[i * CX + depth], cells[i * CX + CX - 1 - depth]
            xa[row:row + NE, :] = jnp.where(px, high, low)
            xb[row:row + NE, :] = jnp.where(px, low, high)
            low, high = cells[depth * CX + i], cells[(CZ - 1 - depth) * CX + i]
            za[row:row + NE, :] = jnp.where(pz, high, low)
            zb[row:row + NE, :] = jnp.where(pz, low, high)


def halo_rows(flag, a_ref, b_ref, count):
    pairs = [(tile(a_ref, i), tile(b_ref, i)) for i in range(count)]
    return [jnp.where(flag, b, a) for a, b in pairs], [jnp.where(flag, a, b) for a, b in pairs]


def place_of(owner_ref, s):
    place = 0
    for t in range(s):
        place = place + (owner_ref[t] == owner_ref[s]).astype(jnp.int32)
    return place


def blank_lanes(owner_any, block_any, send_ref, owner_ref, block_ref, sem):
    fetches = [
        pltpu.make_async_copy(owner_any, owner_ref, sem.at[0]), pltpu.make_async_copy(block_any, block_ref, sem.at[1])
    ]
    for fetch in fetches:
        fetch.start()
    send_ref[...] = jnp.zeros_like(send_ref)
    for fetch in fetches:
        fetch.wait()
    half = lax.broadcasted_iota(jnp.int32, (1, PB), 1) // (PB // CAP)
    for s in range(KS):
        row = pl.ds(owner_ref[s] * LANE + CAP * NE, 1)
        feeds = jnp.broadcast_to(block_ref[s], (1, PB)).astype(jnp.float32)
        send_ref[row, :] = jnp.where(half == place_of(owner_ref, s), feeds, send_ref[row, :])


def own_columns(cr_ref, blank_any, low_ref, high_ref):
    del blank_any
    cells = native(cr_ref)
    for ref, near, deep in ((low_ref, 0, 1), (high_ref, CY - 1, CY - 2)):
        entries = [(4 * zx, cells[zx], near) for zx in range(ZX)] + [(4 * zx + 1, cells[zx], deep) for zx in range(ZX)]
        ref[...] = gather_columns(jnp.zeros((NE, CY), jnp.float32), entries)


def edge_faces(xa, xb, za, zb, low_ref, high_ref, ya_out, yb_out, ea_out, eb_out):
    px, py, pz = even("gx"), even("gy"), even("gz")
    x_low, x_high = halo_rows(px, xa, xb, CZ)
    z_low, z_high = halo_rows(pz, za, zb, CX)
    packs = []
    for ref, near in ((low_ref, 0), (high_ref, CY - 1)):
        entries = []
        for i in range(4):
            entries.append((4 * (i * CX) + 2, x_low[i], near))
            entries.append((4 * (i * CX + CX - 1) + 2, x_high[i], near))
            entries.append((4 * i + 3, z_low[i], near))
            entries.append((4 * ((CZ - 1) * CX + i) + 3, z_high[i], near))
        packs.append(gather_columns(ref[...], entries))
    low, high = packs
    ya_out[0:NE, :] = jnp.where(py, high, low)
    yb_out[0:NE, :] = jnp.where(py, low, high)
    for ref in (ya_out, yb_out):
        ref[NE:2 * NE, :] = jnp.zeros((NE, CY), jnp.float32)
    for i, rows in enumerate((x_low, x_high)):
        ea_out[i * NE:(i + 1) * NE, :] = jnp.where(pz, rows[CZ - 1], rows[0])
        eb_out[i * NE:(i + 1) * NE, :] = jnp.where(pz, rows[0], rows[CZ - 1])


def column(row):
    square = jnp.broadcast_to(row, (NE, NE))
    across = lax.broadcasted_iota(jnp.int32, (NE, NE), 1)
    down = lax.broadcasted_iota(jnp.int32, (NE, NE), 0)
    return jnp.sum(jnp.where(across == down, square, 0.0), axis=1, keepdims=True)


def coefficients(diff_ref, loss_ref):
    return [jnp.broadcast_to(column(ref[...]), (NE, CY)) for ref in (diff_ref, loss_ref)]


def inside(axis):
    at = lax.axis_index(axis)
    return at > 0, at < lax.axis_size(axis) - 1


def stepper(diff, loss):
    top = lax.broadcasted_iota(jnp.int32, (NE, CY), 0) == NE - 1

    def update(c, beside):
        flux = loss * c
        above = jnp.where(top, 0.0, pltpu.roll(flux, NE - 1, 0))
        return c + diff * (beside - 6.0 * c) + above - flux

    return update


def inner_steps(cr_ref, xa, xb, za, zb, diff_ref, loss_ref, inner_ref):
    px, pz = even("gx"), even("gz")
    lane = lanes()
    diff, loss = coefficients(diff_ref, loss_ref)
    update = stepper(diff, loss)
    cells = native(cr_ref)
    x_low, x_high = halo_rows(px, xa, xb, 2 * CZ)
    z_low, z_high = halo_rows(pz, za, zb, 2 * CX)

    def along_y(c):
        return jnp.where(lane == CY - 1, 0.0, pltpu.roll(c, CY - 1, 1)) + jnp.where(lane == 0, 0.0, pltpu.roll(c, 1, 1))

    def at(z, x):
        if 0 <= z < CZ and 0 <= x < CX:
            return cells[z * CX + x]
        if 0 <= z < CZ:
            return x_low[(-1 - x) * CZ + z] if x < 0 else x_high[(x - CX) * CZ + z]
        if 0 <= x < CX:
            return z_low[(-1 - z) * CX + x] if z < 0 else z_high[(z - CZ) * CX + x]
        return None

    def around(get, z, x):
        found = [get(z + 1, x), get(z - 1, x), get(z, x + 1), get(z, x - 1)]
        found = [values for values in found if values is not None]
        return sum(found[1:], found[0])

    now = {}
    for z in range(-1, CZ + 1):
        for x in range(-1, CX + 1):
            if at(z, x) is None:
                continue
            new = around(at, z, x)
            if 0 <= z < CZ and 0 <= x < CX:
                now[z, x] = update(at(z, x), new + along_y(at(z, x)))
            else:
                axis, upper = ("gx", x > 0) if 0 <= z < CZ else ("gz", z > 0)
                now[z, x] = jnp.where(inside(axis)[1 if upper else 0], update(at(z, x), new), 0.0)
    for z in range(CZ):
        for x in range(CX):
            c = now[z, x]
            halos = [at(*there) for there in ((z + 1, x), (z - 1, x), (z, x + 1), (z, x - 1))
                     if not (0 <= there[0] < CZ and 0 <= there[1] < CX)]
            mixed = c + diff * sum(halos[1:], halos[0]) if halos else c
            row = (z * CX + x) * NE
            inner_ref[row:row + NE, :] = update(c, around(lambda *there: now[there], z, x) + along_y(mixed))


def y_corrections(pack, own, diff, loss, update, here):
    place = lax.div(lanes(), 4)
    cx, cz = lax.rem(place, CX), lax.div(place, CX)
    deep, x_edge, z_edge = moved(pack, -1), moved(pack, -2), moved(pack, -3)

    def around(values, x_halo, z_halo):
        return (
            jnp.where(cz == CZ - 1, z_halo, moved(values, -4 * CX)) + jnp.where(cz == 0, z_halo, moved(values, 4 * CX))
            + jnp.where(cx == CX - 1, x_halo, moved(values, -4)) + jnp.where(cx == 0, x_halo, moved(values, 4))
        )

    beyond = jnp.where(here, update(pack, around(pack, x_edge, z_edge) + deep + own), 0.0)
    first = diff * pack
    outer = update(first, around(first, diff * x_edge, diff * z_edge) + beyond)
    return outer, diff * first


def project(owner_any, lanes_any, inner_ref, low_ref, high_ref, ya, yb, ea, eb, diff_ref, loss_ref, gas_ref, weight_ref,
            cells_ref, send_any, parts_ref, blocks_ref, owner_ref, sem, owner_sem):
    del lanes_any
    fetch = pltpu.make_async_copy(owner_any, owner_ref, owner_sem)
    fetch.start()
    py, pz = even("gy"), even("gz")
    lane = lanes()
    diff, loss = coefficients(diff_ref, loss_ref)
    update = stepper(diff, loss)
    e_low, e_high = halo_rows(pz, ea, eb, 2)
    (y_low,), (y_high,) = halo_rows(py, ya, yb, 1)
    below, beyond = inside("gy")
    outer_low, next_low = y_corrections(y_low, low_ref[...], diff, loss, update, below)
    outer_high, next_high = y_corrections(y_high, high_ref[...], diff, loss, update, beyond)
    kind = lax.rem(lane, 4)
    mixed = jnp.where(kind == 0, outer_low, moved(next_low, 1))
    mixed = jnp.where(kind == 3, moved(outer_high, -1), mixed)
    mixed = jnp.where(kind == 2, moved(next_high, -2), mixed)
    rim = (lane < 2) | (lane >= CY - 2)
    corners = {0: e_low[0], CX - 1: e_low[1], (CZ - 1) * CX: e_high[0], ZX - 1: e_high[1]}
    for zx in range(ZX):
        cell = tile(inner_ref, zx) + jnp.where(rim, moved(mixed, -4 * zx), 0.0)
        if zx in corners:
            cell = cell + 2.0 * diff * diff * corners[zx]
        cells_ref[zx * NE:(zx + 1) * NE, :] = cell
        lit = cell * gas_ref[zx:zx + 1, :]
        upper = lit.astype(jnp.bfloat16)
        parts_ref[0:NE, zx * CY:(zx + 1) * CY] = upper
        parts_ref[NE:2 * NE, zx * CY:(zx + 1) * CY] = (lit - upper.astype(jnp.float32)).astype(jnp.bfloat16)
    weights = jnp.concatenate([weight_ref[s] for s in range(KS)], axis=1)
    product = jnp.dot(parts_ref[...], weights, preferred_element_type=jnp.float32)
    product = product[:NE] + product[NE:]
    for s in range(KS):
        blocks_ref[s * NE:(s + 1) * NE, 0, :] = product[:, s * PB:(s + 1) * PB]
    fetch.wait()
    copies = []
    for s in range(KS):
        row = owner_ref[s] * LANE + place_of(owner_ref, s) * NE
        copies.append(pltpu.make_async_copy(blocks_ref.at[pl.ds(s * NE, NE)], send_any.at[pl.ds(row, NE)], sem.at[s]))
        copies[s].start()
    for copy in copies:
        copy.wait()


def finish_density(cells_ref, final_ref):
    for zx in range(ZX):
        final_ref[pl.ds(zx, NE, stride=ZX), :] = tile(cells_ref, zx)


def gather_sky(recv_ref, table_ref, sky_ref):
    count = recv_ref.shape[0] // LANE
    total = [jnp.zeros((NE, PB), jnp.float32) for _ in range(BO)]
    feeds = recv_ref[pl.ds(CAP * NE, count, stride=LANE), :]
    first = lax.broadcasted_iota(jnp.int32, (count, PB), 1) < PB // 2
    turned = pltpu.roll(feeds, PB // 2, 1)
    feeds = [jnp.where(first, feeds, turned), jnp.where(first, turned, feeds)]
    for b in range(BO):
        chosen = [jnp.where(rows == b, 1.0, 0.0) for rows in feeds]
        for j in range(count):
            for k in range(CAP):
                block = recv_ref[j * LANE + k * NE:j * LANE + (k + 1) * NE, :]
                total[b] = total[b] + block * chosen[k][j:j + 1, :]
    for b in range(BO):
        sky_ref[b * NG:(b + 1) * NG, :] = jnp.dot(
            table_ref[...], total[b], precision=lax.Precision.HIGHEST, preferred_element_type=jnp.float32
        )


def f32(*shape):
    return jax.ShapeDtypeStruct(shape, jnp.float32)


def cost(us):
    return pl.CostEstimate(flops=0, transcendentals=0, bytes_accessed=us * 3000000)


def call(body, name, outs, in_specs, us, out_specs=None, scratch=(), aliases=None):
    return pl.pallas_call(
        body,
        name=name,
        out_shape=outs,
        in_specs=in_specs,
        out_specs=out_specs or [VMEM] * len(outs),
        scratch_shapes=list(scratch),
        input_output_aliases=aliases or {},
        cost_estimate=cost(us),
        compiler_params=pltpu.CompilerParams(vmem_limit_bytes=SMALL),
    )


def swap(values, axis, start):
    pairs = []
    for i in range(start, lax.axis_size(axis) - 1, 2):
        pairs += [(i, i + 1), (i + 1, i)]
    return lax.ppermute(values, axis, pairs)


def body(cr_init, gas, diff_coeff, loss_coeff, pi0_table, los_weight, slot_owner, slot_block):
    start = cr_init.reshape(NE * ZX, CY)
    diff, loss = diff_coeff.reshape(1, NE), loss_coeff.reshape(1, NE)
    column_pack, edge_rows = f32(NE, CY), f32(2 * NE, CY)
    xa, xb, za, zb = call(first_faces, "first_faces", [f32(2 * 4 * NE, CY)] * 4, [VMEM], 1)(start)
    xb = swap(xb, "gx", 1)
    xa = swap(xa, "gx", 0)
    za = swap(za, "gz", 0)
    zb = swap(zb, "gz", 1)
    owner, owners = slot_owner.reshape(KS), lax.axis_size("gy")
    (blank,) = call(
        blank_lanes,
        "blank_lanes",
        [f32(owners * LANE, PB)],
        [ANY] * 2,
        1,
        scratch=[pltpu.SMEM((KS,), jnp.int32), pltpu.SMEM((KS,), jnp.int32), pltpu.SemaphoreType.DMA((2,))],
    )(owner, slot_block.reshape(KS))
    low, high = call(own_columns, "own_columns", [column_pack] * 2, [VMEM, ANY], 1)(start, blank)
    ya, yb, ea, eb = call(edge_faces, "edge_faces", [edge_rows] * 4, [VMEM] * 6, 1)(
        xa, xb, za, zb, low, high
    )
    yb = swap(yb, "gy", 1)
    ya = swap(ya, "gy", 0)
    ea = swap(ea, "gz", 0)
    eb = swap(eb, "gz", 1)
    (inner,) = call(inner_steps, "inner_steps", [f32(ZX * NE, CY)], [VMEM] * 7, 2)(start, xa, xb, za, zb, diff, loss)
    cells, send = call(
        project,
        "project",
        [f32(ZX * NE, CY), f32(owners * LANE, 1, PB)],
        [ANY] * 2 + [VMEM] * 11,
        2,
        out_specs=[VMEM, ANY],
        scratch=[
            pltpu.VMEM((2 * NE, ZX * CY), jnp.bfloat16),
            pltpu.VMEM((KS * NE, 1, PB), jnp.float32),
            pltpu.SMEM((KS,), jnp.int32),
            pltpu.SemaphoreType.DMA((KS,)),
            pltpu.SemaphoreType.DMA,
        ],
        aliases={1: 1},
    )(
        owner, blank.reshape(owners * LANE, 1, PB), inner, low, high, ya, yb, ea, eb, diff, loss,
        gas.reshape(ZX, CY), los_weight.reshape(KS, ZX * CY, PB),
    )
    (final,) = call(finish_density, "finish_density", [f32(NE * ZX, CY)], [VMEM], 2)(cells)
    recv = lax.all_to_all(send.reshape(owners, 1, LANE * PB), "gy", 0, 0, tiled=True)
    (sky,) = call(gather_sky, "gather_sky", [f32(BO * NG, PB)], [VMEM] * 2, 1)(
        recv.reshape(owners * LANE, PB), pi0_table
    )
    return final.reshape(cr_init.shape), sky.reshape(1, 1, BO, NG, PB)


def solution(mesh):
    in_specs = (
        P(None, "gz", "gx", "gy"),
        P("gz", "gx", "gy"),
        P(),
        P(),
        P(),
        P("gz", "gx", "gy", None, None, None),
        P("gz", "gx", "gy", None, None),
        P("gz", "gx", "gy", None),
    )
    out_specs = (P(None, "gz", "gx", "gy"), P("gz", "gx", "gy", None, None))
    return jax.shard_map(body, mesh=mesh, in_specs=in_specs, out_specs=out_specs, check_vma=False)
```

```python
import jax
import jax.numpy as jnp
from jax import lax
from jax.experimental import pallas as pl
from jax.experimental.pallas import tpu as pltpu
from jax.sharding import PartitionSpec as P

NE = 64
NG = 96
PB = 128
CX = 4
CZ = 4
CY = 128
KS = 7
BO = 4
CAP = 2
ZX = CZ * CX
LANE = CAP * NE + 1
VMEM = pl.BlockSpec(memory_space=pltpu.VMEM)
ANY = pl.BlockSpec(memory_space=pl.ANY)
SMALL = 16 * 1024 * 1024


def even(axis):
    return lax.rem(lax.axis_index(axis), 2) == 0


def tile(ref, row):
    return ref[row * NE:(row + 1) * NE, :]


def native(ref):
    return [ref[pl.ds(zx, NE, stride=ZX), :] for zx in range(ZX)]


def lanes():
    return lax.broadcasted_iota(jnp.int32, (NE, CY), 1)


def moved(values, shift):
    return values if shift % CY == 0 else pltpu.roll(values, shift % CY, 1)


def gather_columns(packed, entries):
    lane = lanes()
    for to, values, at in entries:
        packed = jnp.where(lane == to, moved(values, to - at), packed)
    return packed


def first_faces(cr_ref, xa, xb, za, zb):
    cells = native(cr_ref)
    px, pz = even("gx"), even("gz")
    for depth in range(2):
        for i in range(4):
            row = (depth * 4 + i) * NE
            low, high = cells[i * CX + depth], cells[i * CX + CX - 1 - depth]
            xa[row:row + NE, :] = jnp.where(px, high, low)
            xb[row:row + NE, :] = jnp.where(px, low, high)
            low, high = cells[depth * CX + i], cells[(CZ - 1 - depth) * CX + i]
            za[row:row + NE, :] = jnp.where(pz, high, low)
            zb[row:row + NE, :] = jnp.where(pz, low, high)


def halo_rows(flag, a_ref, b_ref, count):
    pairs = [(tile(a_ref, i), tile(b_ref, i)) for i in range(count)]
    return [jnp.where(flag, b, a) for a, b in pairs], [jnp.where(flag, a, b) for a, b in pairs]


def place_of(owner_ref, s):
    place = 0
    for t in range(s):
        place = place + (owner_ref[t] == owner_ref[s]).astype(jnp.int32)
    return place


def blank_lanes(owner_any, block_any, send_ref, owner_ref, block_ref, sem):
    fetches = [
        pltpu.make_async_copy(owner_any, owner_ref, sem.at[0]), pltpu.make_async_copy(block_any, block_ref, sem.at[1])
    ]
    for fetch in fetches:
        fetch.start()
    send_ref[...] = jnp.zeros_like(send_ref)
    for fetch in fetches:
        fetch.wait()
    half = lax.broadcasted_iota(jnp.int32, (1, PB), 1) // (PB // CAP)
    for s in range(KS):
        row = pl.ds(owner_ref[s] * LANE + CAP * NE, 1)
        feeds = jnp.broadcast_to(block_ref[s], (1, PB)).astype(jnp.float32)
        send_ref[row, :] = jnp.where(half == place_of(owner_ref, s), feeds, send_ref[row, :])


def own_columns(cr_ref, blank_any, low_ref, high_ref):
    del blank_any
    cells = native(cr_ref)
    for ref, near, deep in ((low_ref, 0, 1), (high_ref, CY - 1, CY - 2)):
        entries = [(4 * zx, cells[zx], near) for zx in range(ZX)] + [(4 * zx + 1, cells[zx], deep) for zx in range(ZX)]
        ref[...] = gather_columns(jnp.zeros((NE, CY), jnp.float32), entries)


def edge_faces(xa, xb, za, zb, low_ref, high_ref, ya_out, yb_out, ea_out, eb_out):
    px, py, pz = even("gx"), even("gy"), even("gz")
    x_low, x_high = halo_rows(px, xa, xb, CZ)
    z_low, z_high = halo_rows(pz, za, zb, CX)
    packs = []
    for ref, near in ((low_ref, 0), (high_ref, CY - 1)):
        entries = []
        for i in range(4):
            entries.append((4 * (i * CX) + 2, x_low[i], near))
            entries.append((4 * (i * CX + CX - 1) + 2, x_high[i], near))
            entries.append((4 * i + 3, z_low[i], near))
            entries.append((4 * ((CZ - 1) * CX + i) + 3, z_high[i], near))
        packs.append(gather_columns(ref[...], entries))
    low, high = packs
    ya_out[0:NE, :] = jnp.where(py, high, low)
    yb_out[0:NE, :] = jnp.where(py, low, high)
    for ref in (ya_out, yb_out):
        ref[NE:2 * NE, :] = jnp.zeros((NE, CY), jnp.float32)
    for i, rows in enumerate((x_low, x_high)):
        ea_out[i * NE:(i + 1) * NE, :] = jnp.where(pz, rows[CZ - 1], rows[0])
        eb_out[i * NE:(i + 1) * NE, :] = jnp.where(pz, rows[0], rows[CZ - 1])


def column(row):
    square = jnp.broadcast_to(row, (NE, NE))
    across = lax.broadcasted_iota(jnp.int32, (NE, NE), 1)
    down = lax.broadcasted_iota(jnp.int32, (NE, NE), 0)
    return jnp.sum(jnp.where(across == down, square, 0.0), axis=1, keepdims=True)


def coefficients(diff_ref, loss_ref):
    return [jnp.broadcast_to(column(ref[...]), (NE, CY)) for ref in (diff_ref, loss_ref)]


def inside(axis):
    at = lax.axis_index(axis)
    return at > 0, at < lax.axis_size(axis) - 1


def stepper(diff, loss):
    top = lax.broadcasted_iota(jnp.int32, (NE, CY), 0) == NE - 1
    keep = 1.0 - 6.0 * diff - loss
    loss_above = jnp.where(top, 0.0, pltpu.roll(loss, NE - 1, 0))

    def update(c, beside):
        return keep * c + diff * beside + loss_above * pltpu.roll(c, NE - 1, 0)

    return update


def inner_steps(cr_ref, xa, xb, za, zb, diff_ref, loss_ref, inner_ref):
    px, pz = even("gx"), even("gz")
    lane = lanes()
    diff, loss = coefficients(diff_ref, loss_ref)
    update = stepper(diff, loss)
    cells = native(cr_ref)
    x_low, x_high = halo_rows(px, xa, xb, 2 * CZ)
    z_low, z_high = halo_rows(pz, za, zb, 2 * CX)

    def along_y(c):
        return jnp.where(lane == CY - 1, 0.0, pltpu.roll(c, CY - 1, 1)) + jnp.where(lane == 0, 0.0, pltpu.roll(c, 1, 1))

    def at(z, x):
        if 0 <= z < CZ and 0 <= x < CX:
            return cells[z * CX + x]
        if 0 <= z < CZ:
            return x_low[(-1 - x) * CZ + z] if x < 0 else x_high[(x - CX) * CZ + z]
        if 0 <= x < CX:
            return z_low[(-1 - z) * CX + x] if z < 0 else z_high[(z - CZ) * CX + x]
        return None

    def around(get, z, x):
        found = [get(z + 1, x), get(z - 1, x), get(z, x + 1), get(z, x - 1)]
        found = [values for values in found if values is not None]
        return sum(found[1:], found[0])

    now = {}
    for z in range(-1, CZ + 1):
        for x in range(-1, CX + 1):
            if at(z, x) is None:
                continue
            new = around(at, z, x)
            if 0 <= z < CZ and 0 <= x < CX:
                now[z, x] = update(at(z, x), new + along_y(at(z, x)))
            else:
                axis, upper = ("gx", x > 0) if 0 <= z < CZ else ("gz", z > 0)
                now[z, x] = jnp.where(inside(axis)[1 if upper else 0], update(at(z, x), new), 0.0)
    for z in range(CZ):
        for x in range(CX):
            c = now[z, x]
            halos = [at(*there) for there in ((z + 1, x), (z - 1, x), (z, x + 1), (z, x - 1))
                     if not (0 <= there[0] < CZ and 0 <= there[1] < CX)]
            mixed = c + diff * sum(halos[1:], halos[0]) if halos else c
            row = (z * CX + x) * NE
            inner_ref[row:row + NE, :] = update(c, around(lambda *there: now[there], z, x) + along_y(mixed))


def y_corrections(pack, own, diff, loss, update, here):
    place = lax.div(lanes(), 4)
    cx, cz = lax.rem(place, CX), lax.div(place, CX)
    deep, x_edge, z_edge = moved(pack, -1), moved(pack, -2), moved(pack, -3)

    def around(values, x_halo, z_halo):
        return (
            jnp.where(cz == CZ - 1, z_halo, moved(values, -4 * CX)) + jnp.where(cz == 0, z_halo, moved(values, 4 * CX))
            + jnp.where(cx == CX - 1, x_halo, moved(values, -4)) + jnp.where(cx == 0, x_halo, moved(values, 4))
        )

    beyond = jnp.where(here, update(pack, around(pack, x_edge, z_edge) + deep + own), 0.0)
    first = diff * pack
    outer = update(first, around(first, diff * x_edge, diff * z_edge) + beyond)
    return outer, diff * first


def project(owner_any, lanes_any, inner_ref, low_ref, high_ref, ya, yb, ea, eb, diff_ref, loss_ref, gas_ref, weight_ref,
            cells_ref, send_any, parts_ref, blocks_ref, owner_ref, sem, owner_sem):
    del lanes_any
    fetch = pltpu.make_async_copy(owner_any, owner_ref, owner_sem)
    fetch.start()
    py, pz = even("gy"), even("gz")
    lane = lanes()
    diff, loss = coefficients(diff_ref, loss_ref)
    update = stepper(diff, loss)
    e_low, e_high = halo_rows(pz, ea, eb, 2)
    (y_low,), (y_high,) = halo_rows(py, ya, yb, 1)
    below, beyond = inside("gy")
    outer_low, next_low = y_corrections(y_low, low_ref[...], diff, loss, update, below)
    outer_high, next_high = y_corrections(y_high, high_ref[...], diff, loss, update, beyond)
    kind = lax.rem(lane, 4)
    mixed = jnp.where(kind == 0, outer_low, moved(next_low, 1))
    mixed = jnp.where(kind == 3, moved(outer_high, -1), mixed)
    mixed = jnp.where(kind == 2, moved(next_high, -2), mixed)
    rim = (lane < 2) | (lane >= CY - 2)
    corners = {0: e_low[0], CX - 1: e_low[1], (CZ - 1) * CX: e_high[0], ZX - 1: e_high[1]}
    for zx in range(ZX):
        cell = tile(inner_ref, zx) + jnp.where(rim, moved(mixed, -4 * zx), 0.0)
        if zx in corners:
            cell = cell + 2.0 * diff * diff * corners[zx]
        cells_ref[zx * NE:(zx + 1) * NE, :] = cell
        lit = cell * gas_ref[zx:zx + 1, :]
        upper = lit.astype(jnp.bfloat16)
        parts_ref[0:NE, zx * CY:(zx + 1) * CY] = upper
        parts_ref[NE:2 * NE, zx * CY:(zx + 1) * CY] = (lit - upper.astype(jnp.float32)).astype(jnp.bfloat16)
    weights = jnp.concatenate([weight_ref[s] for s in range(KS)], axis=1)
    product = jnp.dot(parts_ref[...], weights, preferred_element_type=jnp.float32)
    product = product[:NE] + product[NE:]
    for s in range(KS):
        blocks_ref[s * NE:(s + 1) * NE, 0, :] = product[:, s * PB:(s + 1) * PB]
    fetch.wait()
    copies = []
    for s in range(KS):
        row = owner_ref[s] * LANE + place_of(owner_ref, s) * NE
        copies.append(pltpu.make_async_copy(blocks_ref.at[pl.ds(s * NE, NE)], send_any.at[pl.ds(row, NE)], sem.at[s]))
        copies[s].start()
    for copy in copies:
        copy.wait()


def finish_density(cells_ref, final_ref):
    for zx in range(ZX):
        final_ref[pl.ds(zx, NE, stride=ZX), :] = tile(cells_ref, zx)


def gather_sky(recv_ref, table_ref, sky_ref):
    count = recv_ref.shape[0] // LANE
    total = [jnp.zeros((NE, PB), jnp.float32) for _ in range(BO)]
    feeds = recv_ref[pl.ds(CAP * NE, count, stride=LANE), :]
    first = lax.broadcasted_iota(jnp.int32, (count, PB), 1) < PB // 2
    turned = pltpu.roll(feeds, PB // 2, 1)
    feeds = [jnp.where(first, feeds, turned), jnp.where(first, turned, feeds)]
    for b in range(BO):
        chosen = [jnp.where(rows == b, 1.0, 0.0) for rows in feeds]
        for j in range(count):
            for k in range(CAP):
                block = recv_ref[j * LANE + k * NE:j * LANE + (k + 1) * NE, :]
                total[b] = total[b] + block * chosen[k][j:j + 1, :]
    for b in range(BO):
        sky_ref[b * NG:(b + 1) * NG, :] = jnp.dot(
            table_ref[...], total[b], precision=lax.Precision.HIGHEST, preferred_element_type=jnp.float32
        )


def f32(*shape):
    return jax.ShapeDtypeStruct(shape, jnp.float32)


def cost(us):
    return pl.CostEstimate(flops=0, transcendentals=0, bytes_accessed=us * 3000000)


def call(body, name, outs, in_specs, us, out_specs=None, scratch=(), aliases=None):
    return pl.pallas_call(
        body,
        name=name,
        out_shape=outs,
        in_specs=in_specs,
        out_specs=out_specs or [VMEM] * len(outs),
        scratch_shapes=list(scratch),
        input_output_aliases=aliases or {},
        cost_estimate=cost(us),
        compiler_params=pltpu.CompilerParams(vmem_limit_bytes=SMALL),
    )


def swap(values, axis, start):
    pairs = []
    for i in range(start, lax.axis_size(axis) - 1, 2):
        pairs += [(i, i + 1), (i + 1, i)]
    return lax.ppermute(values, axis, pairs)


def body(cr_init, gas, diff_coeff, loss_coeff, pi0_table, los_weight, slot_owner, slot_block):
    start = cr_init.reshape(NE * ZX, CY)
    diff, loss = diff_coeff.reshape(1, NE), loss_coeff.reshape(1, NE)
    column_pack, edge_rows = f32(NE, CY), f32(2 * NE, CY)
    xa, xb, za, zb = call(first_faces, "first_faces", [f32(2 * 4 * NE, CY)] * 4, [VMEM], 1)(start)
    xb = swap(xb, "gx", 1)
    xa = swap(xa, "gx", 0)
    za = swap(za, "gz", 0)
    zb = swap(zb, "gz", 1)
    owner, owners = slot_owner.reshape(KS), lax.axis_size("gy")
    (blank,) = call(
        blank_lanes,
        "blank_lanes",
        [f32(owners * LANE, PB)],
        [ANY] * 2,
        1,
        scratch=[pltpu.SMEM((KS,), jnp.int32), pltpu.SMEM((KS,), jnp.int32), pltpu.SemaphoreType.DMA((2,))],
    )(owner, slot_block.reshape(KS))
    low, high = call(own_columns, "own_columns", [column_pack] * 2, [VMEM, ANY], 1)(start, blank)
    ya, yb, ea, eb = call(edge_faces, "edge_faces", [edge_rows] * 4, [VMEM] * 6, 1)(
        xa, xb, za, zb, low, high
    )
    yb = swap(yb, "gy", 1)
    ya = swap(ya, "gy", 0)
    ea = swap(ea, "gz", 0)
    eb = swap(eb, "gz", 1)
    (inner,) = call(inner_steps, "inner_steps", [f32(ZX * NE, CY)], [VMEM] * 7, 2)(start, xa, xb, za, zb, diff, loss)
    cells, send = call(
        project,
        "project",
        [f32(ZX * NE, CY), f32(owners * LANE, 1, PB)],
        [ANY] * 2 + [VMEM] * 11,
        2,
        out_specs=[VMEM, ANY],
        scratch=[
            pltpu.VMEM((2 * NE, ZX * CY), jnp.bfloat16),
            pltpu.VMEM((KS * NE, 1, PB), jnp.float32),
            pltpu.SMEM((KS,), jnp.int32),
            pltpu.SemaphoreType.DMA((KS,)),
            pltpu.SemaphoreType.DMA,
        ],
        aliases={1: 1},
    )(
        owner, blank.reshape(owners * LANE, 1, PB), inner, low, high, ya, yb, ea, eb, diff, loss,
        gas.reshape(ZX, CY), los_weight.reshape(KS, ZX * CY, PB),
    )
    (final,) = call(finish_density, "finish_density", [f32(NE * ZX, CY)], [VMEM], 2)(cells)
    recv = lax.all_to_all(send.reshape(owners, 1, LANE * PB), "gy", 0, 0, tiled=True)
    (sky,) = call(gather_sky, "gather_sky", [f32(BO * NG, PB)], [VMEM] * 2, 1)(
        recv.reshape(owners * LANE, PB), pi0_table
    )
    return final.reshape(cr_init.shape), sky.reshape(1, 1, BO, NG, PB)


def solution(mesh):
    in_specs = (
        P(None, "gz", "gx", "gy"),
        P("gz", "gx", "gy"),
        P(),
        P(),
        P(),
        P("gz", "gx", "gy", None, None, None),
        P("gz", "gx", "gy", None, None),
        P("gz", "gx", "gy", None),
    )
    out_specs = (P(None, "gz", "gx", "gy"), P("gz", "gx", "gy", None, None))
    return jax.shard_map(body, mesh=mesh, in_specs=in_specs, out_specs=out_specs, check_vma=False)
```

```python
import jax
import jax.numpy as jnp
from jax import lax
from jax.experimental import pallas as pl
from jax.experimental.pallas import tpu as pltpu
from jax.sharding import PartitionSpec as P

NE = 64
NG = 96
PB = 128
CX = 4
CZ = 4
CY = 128
KS = 7
BO = 4
CAP = 2
ZX = CZ * CX
LANE = CAP * NE + 1
VMEM = pl.BlockSpec(memory_space=pltpu.VMEM)
ANY = pl.BlockSpec(memory_space=pl.ANY)
SMALL = 16 * 1024 * 1024


def even(axis):
    return lax.rem(lax.axis_index(axis), 2) == 0


def tile(ref, row):
    return ref[row * NE:(row + 1) * NE, :]


def native(ref):
    return [ref[pl.ds(zx, NE, stride=ZX), :] for zx in range(ZX)]


def lanes():
    return lax.broadcasted_iota(jnp.int32, (NE, CY), 1)


def moved(values, shift):
    return values if shift % CY == 0 else pltpu.roll(values, shift % CY, 1)


def gather_columns(packed, entries):
    lane = lanes()
    for to, values, at in entries:
        packed = jnp.where(lane == to, moved(values, to - at), packed)
    return packed


def first_faces(cr_ref, xa, xb, za, zb):
    cells = native(cr_ref)
    px, pz = even("gx"), even("gz")
    for depth in range(2):
        for i in range(4):
            row = (depth * 4 + i) * NE
            low, high = cells[i * CX + depth], cells[i * CX + CX - 1 - depth]
            xa[row:row + NE, :] = jnp.where(px, high, low)
            xb[row:row + NE, :] = jnp.where(px, low, high)
            low, high = cells[depth * CX + i], cells[(CZ - 1 - depth) * CX + i]
            za[row:row + NE, :] = jnp.where(pz, high, low)
            zb[row:row + NE, :] = jnp.where(pz, low, high)


def halo_rows(flag, a_ref, b_ref, count):
    pairs = [(tile(a_ref, i), tile(b_ref, i)) for i in range(count)]
    return [jnp.where(flag, b, a) for a, b in pairs], [jnp.where(flag, a, b) for a, b in pairs]


def place_of(owner_ref, s):
    place = 0
    for t in range(s):
        place = place + (owner_ref[t] == owner_ref[s]).astype(jnp.int32)
    return place


def blank_lanes(owner_any, block_any, send_ref, owner_ref, block_ref, sem):
    fetches = [
        pltpu.make_async_copy(owner_any, owner_ref, sem.at[0]), pltpu.make_async_copy(block_any, block_ref, sem.at[1])
    ]
    for fetch in fetches:
        fetch.start()
    send_ref[...] = jnp.zeros_like(send_ref)
    for fetch in fetches:
        fetch.wait()
    half = lax.broadcasted_iota(jnp.int32, (1, PB), 1) // (PB // CAP)
    for s in range(KS):
        row = pl.ds(owner_ref[s] * LANE + CAP * NE, 1)
        feeds = jnp.broadcast_to(block_ref[s], (1, PB)).astype(jnp.float32)
        send_ref[row, :] = jnp.where(half == place_of(owner_ref, s), feeds, send_ref[row, :])


def own_columns(cr_ref, blank_any, low_ref, high_ref):
    del blank_any
    cells = native(cr_ref)
    for ref, near, deep in ((low_ref, 0, 1), (high_ref, CY - 1, CY - 2)):
        entries = [(4 * zx, cells[zx], near) for zx in range(ZX)] + [(4 * zx + 1, cells[zx], deep) for zx in range(ZX)]
        ref[...] = gather_columns(jnp.zeros((NE, CY), jnp.float32), entries)


def edge_faces(xa, xb, za, zb, low_ref, high_ref, ya_out, yb_out, ea_out, eb_out):
    px, py, pz = even("gx"), even("gy"), even("gz")
    x_low, x_high = halo_rows(px, xa, xb, CZ)
    z_low, z_high = halo_rows(pz, za, zb, CX)
    packs = []
    for ref, near in ((low_ref, 0), (high_ref, CY - 1)):
        entries = []
        for i in range(4):
            entries.append((4 * (i * CX) + 2, x_low[i], near))
            entries.append((4 * (i * CX + CX - 1) + 2, x_high[i], near))
            entries.append((4 * i + 3, z_low[i], near))
            entries.append((4 * ((CZ - 1) * CX + i) + 3, z_high[i], near))
        packs.append(gather_columns(ref[...], entries))
    low, high = packs
    ya_out[0:NE, :] = jnp.where(py, high, low)
    yb_out[0:NE, :] = jnp.where(py, low, high)
    for ref in (ya_out, yb_out):
        ref[NE:2 * NE, :] = jnp.zeros((NE, CY), jnp.float32)
    for i, rows in enumerate((x_low, x_high)):
        ea_out[i * NE:(i + 1) * NE, :] = jnp.where(pz, rows[CZ - 1], rows[0])
        eb_out[i * NE:(i + 1) * NE, :] = jnp.where(pz, rows[0], rows[CZ - 1])


def column(row):
    square = jnp.broadcast_to(row, (NE, NE))
    across = lax.broadcasted_iota(jnp.int32, (NE, NE), 1)
    down = lax.broadcasted_iota(jnp.int32, (NE, NE), 0)
    return jnp.sum(jnp.where(across == down, square, 0.0), axis=1, keepdims=True)


def coefficients(diff_ref, loss_ref):
    return [jnp.broadcast_to(column(ref[...]), (NE, CY)) for ref in (diff_ref, loss_ref)]


def inside(axis):
    at = lax.axis_index(axis)
    return at > 0, at < lax.axis_size(axis) - 1


def stepper(diff, loss):
    top = lax.broadcasted_iota(jnp.int32, (NE, CY), 0) == NE - 1

    def update(c, beside):
        flux = loss * c
        above = jnp.where(top, 0.0, pltpu.roll(flux, NE - 1, 0))
        return c + diff * (beside - 6.0 * c) + above - flux

    return update


def inner_steps(cr_ref, xa, xb, za, zb, diff_ref, loss_ref, inner_ref):
    px, pz = even("gx"), even("gz")
    lane = lanes()
    diff, loss = coefficients(diff_ref, loss_ref)
    update = stepper(diff, loss)
    cells = native(cr_ref)
    x_low, x_high = halo_rows(px, xa, xb, 2 * CZ)
    z_low, z_high = halo_rows(pz, za, zb, 2 * CX)

    def along_y(c):
        return jnp.where(lane == CY - 1, 0.0, pltpu.roll(c, CY - 1, 1)) + jnp.where(lane == 0, 0.0, pltpu.roll(c, 1, 1))

    def at(z, x):
        if 0 <= z < CZ and 0 <= x < CX:
            return cells[z * CX + x]
        if 0 <= z < CZ:
            return x_low[(-1 - x) * CZ + z] if x < 0 else x_high[(x - CX) * CZ + z]
        if 0 <= x < CX:
            return z_low[(-1 - z) * CX + x] if z < 0 else z_high[(z - CZ) * CX + x]
        return None

    def around(get, z, x):
        found = [get(z + 1, x), get(z - 1, x), get(z, x + 1), get(z, x - 1)]
        found = [values for values in found if values is not None]
        return sum(found[1:], found[0])

    now = {}
    for z in range(-1, CZ + 1):
        for x in range(-1, CX + 1):
            if at(z, x) is None:
                continue
            new = around(at, z, x)
            if 0 <= z < CZ and 0 <= x < CX:
                now[z, x] = update(at(z, x), new + along_y(at(z, x)))
            else:
                axis, upper = ("gx", x > 0) if 0 <= z < CZ else ("gz", z > 0)
                now[z, x] = jnp.where(inside(axis)[1 if upper else 0], update(at(z, x), new), 0.0)
    for z in range(CZ):
        for x in range(CX):
            c = now[z, x]
            halos = [at(*there) for there in ((z + 1, x), (z - 1, x), (z, x + 1), (z, x - 1))
                     if not (0 <= there[0] < CZ and 0 <= there[1] < CX)]
            mixed = c + diff * sum(halos[1:], halos[0]) if halos else c
            row = (z * CX + x) * NE
            inner_ref[row:row + NE, :] = update(c, around(lambda *there: now[there], z, x) + along_y(mixed))


def y_corrections(pack, own, diff, loss, update, here):
    place = lax.div(lanes(), 4)
    cx, cz = lax.rem(place, CX), lax.div(place, CX)
    deep, x_edge, z_edge = moved(pack, -1), moved(pack, -2), moved(pack, -3)

    def around(values, x_halo, z_halo):
        return (
            jnp.where(cz == CZ - 1, z_halo, moved(values, -4 * CX)) + jnp.where(cz == 0, z_halo, moved(values, 4 * CX))
            + jnp.where(cx == CX - 1, x_halo, moved(values, -4)) + jnp.where(cx == 0, x_halo, moved(values, 4))
        )

    beyond = jnp.where(here, update(pack, around(pack, x_edge, z_edge) + deep + own), 0.0)
    first = diff * pack
    outer = update(first, around(first, diff * x_edge, diff * z_edge) + beyond)
    return outer, diff * first


def project(owner_any, lanes_any, inner_ref, low_ref, high_ref, ya, yb, ea, eb, diff_ref, loss_ref, gas_ref, weight_ref,
            cells_ref, send_any, parts_ref, blocks_ref, owner_ref, sem, owner_sem):
    del lanes_any
    fetch = pltpu.make_async_copy(owner_any, owner_ref, owner_sem)
    fetch.start()
    py, pz = even("gy"), even("gz")
    lane = lanes()
    diff, loss = coefficients(diff_ref, loss_ref)
    update = stepper(diff, loss)
    e_low, e_high = halo_rows(pz, ea, eb, 2)
    (y_low,), (y_high,) = halo_rows(py, ya, yb, 1)
    below, beyond = inside("gy")
    outer_low, next_low = y_corrections(y_low, low_ref[...], diff, loss, update, below)
    outer_high, next_high = y_corrections(y_high, high_ref[...], diff, loss, update, beyond)
    kind = lax.rem(lane, 4)
    mixed = jnp.where(kind == 0, outer_low, moved(next_low, 1))
    mixed = jnp.where(kind == 3, moved(outer_high, -1), mixed)
    mixed = jnp.where(kind == 2, moved(next_high, -2), mixed)
    rim = (lane < 2) | (lane >= CY - 2)
    corners = {0: e_low[0], CX - 1: e_low[1], (CZ - 1) * CX: e_high[0], ZX - 1: e_high[1]}
    for zx in range(ZX):
        cell = tile(inner_ref, zx) + jnp.where(rim, moved(mixed, -4 * zx), 0.0)
        if zx in corners:
            cell = cell + 2.0 * diff * diff * corners[zx]
        cells_ref[zx * NE:(zx + 1) * NE, :] = cell
        lit = cell * gas_ref[zx:zx + 1, :]
        upper = lit.astype(jnp.bfloat16)
        parts_ref[0:NE, zx * CY:(zx + 1) * CY] = upper
        parts_ref[NE:2 * NE, zx * CY:(zx + 1) * CY] = (lit - upper.astype(jnp.float32)).astype(jnp.bfloat16)
    weights = jnp.concatenate([weight_ref[s] for s in range(KS)], axis=1)
    product = jnp.dot(parts_ref[...], weights, preferred_element_type=jnp.float32)
    product = product[:NE] + product[NE:]
    for s in range(KS):
        blocks_ref[s * NE:(s + 1) * NE, 0, :] = product[:, s * PB:(s + 1) * PB]
    fetch.wait()
    copies = []
    for s in range(KS):
        row = owner_ref[s] * LANE + place_of(owner_ref, s) * NE
        copies.append(pltpu.make_async_copy(blocks_ref.at[pl.ds(s * NE, NE)], send_any.at[pl.ds(row, NE)], sem.at[s]))
        copies[s].start()
    for copy in copies:
        copy.wait()


def finish_density(cells_ref, final_ref):
    for zx in range(ZX):
        final_ref[pl.ds(zx, NE, stride=ZX), :] = tile(cells_ref, zx)


def gather_sky(recv_ref, table_ref, sky_any, total_ref, sky_ref, sem):
    count = recv_ref.shape[0] // LANE
    feeds = recv_ref[pl.ds(CAP * NE, count, stride=LANE), :]
    first = lax.broadcasted_iota(jnp.int32, (count, PB), 1) < PB // 2
    turned = pltpu.roll(feeds, PB // 2, 1)
    feeds = [jnp.where(first, feeds, turned), jnp.where(first, turned, feeds)]
    chosen = [[jnp.where(rows == b, 1.0, 0.0) for b in range(BO)] for rows in feeds]
    part = NE // 2
    for at in range(0, NE, part):
        total = [jnp.zeros((part, PB), jnp.float32) for _ in range(BO)]
        for j in range(count):
            for k in range(CAP):
                row = j * LANE + k * NE + at
                block = recv_ref[row:row + part, :]
                for b in range(BO):
                    total[b] = total[b] + block * chosen[k][b][j:j + 1, :]
        for b in range(BO):
            total_ref[b * NE + at:b * NE + at + part, :] = total[b]
    copies = []
    for b in range(BO):
        sky_ref[b * NG:(b + 1) * NG, :] = jnp.dot(
            table_ref[...], tile(total_ref, b), precision=lax.Precision.HIGHEST, preferred_element_type=jnp.float32
        )
        rows = pl.ds(b * NG, NG)
        copies.append(pltpu.make_async_copy(sky_ref.at[rows], sky_any.at[rows], sem.at[b]))
        copies[b].start()
    for copy in copies:
        copy.wait()


def f32(*shape):
    return jax.ShapeDtypeStruct(shape, jnp.float32)


def cost(us):
    return pl.CostEstimate(flops=0, transcendentals=0, bytes_accessed=us * 3000000)


def call(body, name, outs, in_specs, us, out_specs=None, scratch=(), aliases=None):
    return pl.pallas_call(
        body,
        name=name,
        out_shape=outs,
        in_specs=in_specs,
        out_specs=out_specs or [VMEM] * len(outs),
        scratch_shapes=list(scratch),
        input_output_aliases=aliases or {},
        cost_estimate=cost(us),
        compiler_params=pltpu.CompilerParams(vmem_limit_bytes=SMALL),
    )


def swap(values, axis, start):
    pairs = []
    for i in range(start, lax.axis_size(axis) - 1, 2):
        pairs += [(i, i + 1), (i + 1, i)]
    return lax.ppermute(values, axis, pairs)


def body(cr_init, gas, diff_coeff, loss_coeff, pi0_table, los_weight, slot_owner, slot_block):
    start = cr_init.reshape(NE * ZX, CY)
    diff, loss = diff_coeff.reshape(1, NE), loss_coeff.reshape(1, NE)
    column_pack, edge_rows = f32(NE, CY), f32(2 * NE, CY)
    xa, xb, za, zb = call(first_faces, "first_faces", [f32(2 * 4 * NE, CY)] * 4, [VMEM], 1)(start)
    xb = swap(xb, "gx", 1)
    xa = swap(xa, "gx", 0)
    za = swap(za, "gz", 0)
    zb = swap(zb, "gz", 1)
    owner, owners = slot_owner.reshape(KS), lax.axis_size("gy")
    (blank,) = call(
        blank_lanes,
        "blank_lanes",
        [f32(owners * LANE, PB)],
        [ANY] * 2,
        1,
        scratch=[pltpu.SMEM((KS,), jnp.int32), pltpu.SMEM((KS,), jnp.int32), pltpu.SemaphoreType.DMA((2,))],
    )(owner, slot_block.reshape(KS))
    low, high = call(own_columns, "own_columns", [column_pack] * 2, [VMEM, ANY], 1)(start, blank)
    ya, yb, ea, eb = call(edge_faces, "edge_faces", [edge_rows] * 4, [VMEM] * 6, 1)(
        xa, xb, za, zb, low, high
    )
    yb = swap(yb, "gy", 1)
    ya = swap(ya, "gy", 0)
    ea = swap(ea, "gz", 0)
    eb = swap(eb, "gz", 1)
    (inner,) = call(inner_steps, "inner_steps", [f32(ZX * NE, CY)], [VMEM] * 7, 2)(start, xa, xb, za, zb, diff, loss)
    cells, send = call(
        project,
        "project",
        [f32(ZX * NE, CY), f32(owners * LANE, 1, PB)],
        [ANY] * 2 + [VMEM] * 11,
        2,
        out_specs=[VMEM, ANY],
        scratch=[
            pltpu.VMEM((2 * NE, ZX * CY), jnp.bfloat16),
            pltpu.VMEM((KS * NE, 1, PB), jnp.float32),
            pltpu.SMEM((KS,), jnp.int32),
            pltpu.SemaphoreType.DMA((KS,)),
            pltpu.SemaphoreType.DMA,
        ],
        aliases={1: 1},
    )(
        owner, blank.reshape(owners * LANE, 1, PB), inner, low, high, ya, yb, ea, eb, diff, loss,
        gas.reshape(ZX, CY), los_weight.reshape(KS, ZX * CY, PB),
    )
    (final,) = call(finish_density, "finish_density", [f32(NE * ZX, CY)], [VMEM], 2)(cells)
    recv = lax.all_to_all(send.reshape(owners, 1, LANE * PB), "gy", 0, 0, tiled=True)
    (sky,) = call(
        gather_sky,
        "gather_sky",
        [f32(BO * NG, PB)],
        [VMEM] * 2,
        1,
        out_specs=[ANY],
        scratch=[
            pltpu.VMEM((BO * NE, PB), jnp.float32), pltpu.VMEM((BO * NG, PB), jnp.float32), pltpu.SemaphoreType.DMA((BO,))
        ],
    )(
        recv.reshape(owners * LANE, PB), pi0_table
    )
    return final.reshape(cr_init.shape), sky.reshape(1, 1, BO, NG, PB)


def solution(mesh):
    in_specs = (
        P(None, "gz", "gx", "gy"),
        P("gz", "gx", "gy"),
        P(),
        P(),
        P(),
        P("gz", "gx", "gy", None, None, None),
        P("gz", "gx", "gy", None, None),
        P("gz", "gx", "gy", None),
    )
    out_specs = (P(None, "gz", "gx", "gy"), P("gz", "gx", "gy", None, None))
    return jax.shard_map(body, mesh=mesh, in_specs=in_specs, out_specs=out_specs, check_vma=False)
```
